32 devices in a mesh: bank: 8 (over y, x, core), blk: 4 (over z).
Axes of the slice: x: 2, y: 2, z: 4, core: 2. Of those that a mesh axis runs over, the one named last changes fastest.
Arguments:
- self_queries: bfloat16 [8, 768, 1024], P('bank', 'blk'), may hold values from -8 to 8
- cache_keys: bfloat16 [8, 1536, 1024], P('bank', 'blk'), may hold values from -8 to 8
- cache_values: bfloat16 [8, 1536, 1024], P('bank', 'blk'), may hold values from -6 to 6
- cache_lengths: int32 [8, 4], P('bank', 'blk'), may hold values from 2 to 384
- cross_queries: bfloat16 [8, 768, 1024], P('bank', 'blk'), may hold values from -8 to 8
- bank_kv: bfloat16 [16, 64, 2048], P('bank'), may hold values from -8 to 8
- span_home: int32 [16], replicated, may hold values from 0 to 15, as said below
- neighbours: int32 [8, 48, 2], P('bank', 'blk'), may hold values from 0 to 15, as said below
Outputs:
- context_out: bfloat16 [8, 768, 1024], P('bank', 'blk')
- retrieved_out: bfloat16 [8, 768, 1024], P('bank', 'blk')
The draws below stay inside these ranges and needn't reach their ends.
Inputs may be any that keep to these rules, and one draw needn't show every extreme that they name: `span_home`: a permutation of the span ids. `neighbours`: of the 24 ids of one device, at most 3 have span_home[id] // 2 equal to any one bank index, and on every device some bank index is named exactly 3 times.
All inputs are finite; a program needn't handle non-finite values.
Results may differ from the reference program's by a relative error of at most 0.0048.
Values may be sent and summed in bfloat16 or wider, within the bound.
No kernel may reach another device: no remote copies, remote signals or barrier semaphores. Data moves between devices by JAX's collectives and lax.ppermute only.
A program may use at most 64 MiB of HBM per device.

```python
import jax
import jax.numpy as jnp
from jax import lax

HEADS = 8
HD = 128
KVW = 1024
SPAN = 16
NROW = 64
NEIGH = 2
BANK_DEV = 2
CACHE_DEV = 384
NCH_DEV = 12
CAP = 3
SESSION = 1536
QROWS = 768
QCH = 48
N_BANK = 8
N_BLK = 4


def drawn_queries(key, salt):
    shape = (N_BANK, N_BLK * NCH_DEV * SPAN, HEADS * HD)
    inner = jax.random.fold_in(key, salt)
    base = 2.0 * jax.random.truncated_normal(inner, -4.0, 4.0, shape, jnp.float32)
    return base.astype(jnp.bfloat16)


def drawn_keys(key, salt, shape):
    inner = jax.random.fold_in(key, salt)
    base = 2.0 * jax.random.truncated_normal(inner, -4.0, 4.0, shape, jnp.float32)
    return base


def draw_self_queries(key, part):
    return drawn_queries(key, 11)


def draw_cross_queries(key, part):
    return drawn_queries(key, 13)


def draw_cache_keys(key, part):
    shape = (N_BANK, N_BLK * CACHE_DEV, HEADS * HD)
    return drawn_keys(key, 19, shape).astype(jnp.bfloat16)


def draw_bank_kv(key, part):
    shape = (BANK_DEV * N_BANK, NROW, HEADS * HD)
    keys_part = drawn_keys(key, 23, shape)
    values_part = jax.random.truncated_normal(jax.random.fold_in(key, 29), -6.0, 6.0, shape, jnp.float32)
    return jnp.concatenate((keys_part, values_part), axis=2).astype(jnp.bfloat16)


def draw_cache_lengths(key, part):
    drawn = jax.random.randint(jax.random.fold_in(key, 17), (N_BANK, N_BLK), 2, CACHE_DEV + 1)
    full = jnp.arange(N_BLK)[None, :] == (jnp.arange(N_BANK) % N_BLK)[:, None]
    return jnp.where(full, CACHE_DEV, drawn).astype(jnp.int32)


def home_table(key):
    return jax.random.permutation(jax.random.fold_in(key, 31), BANK_DEV * N_BANK).astype(jnp.int32)


def draw_span_home(key, part):
    return home_table(key)


def draw_neighbours(key, part):
    readers = N_BANK * N_BLK
    places = N_BANK * CAP
    wanted = NCH_DEV * NEIGH
    owner_of = jnp.arange(places, dtype=jnp.int32) // CAP
    heat = jax.random.randint(jax.random.fold_in(key, 41), (N_BANK,), 0, 4) * 32768
    noise = jax.random.randint(jax.random.fold_in(key, 43), (readers, places), 0, 32768)
    score = (noise + heat[owner_of][None, :]) * places + jnp.arange(places, dtype=jnp.int32)[None, :]
    order = jnp.argsort(score, axis=1)
    picked = owner_of[order[:, :wanted]]
    if CAP == 2:
        first = picked[:, 0]
        twice = jnp.sum((picked == first[:, None]).astype(jnp.int32), axis=1) >= 2
        final = jnp.where(twice, picked[:, wanted - 1], first)
        picked = picked.at[:, wanted - 1].set(final)
    within = jax.random.randint(jax.random.fold_in(key, 47), (readers, wanted), 0, BANK_DEV)
    inverse = jnp.argsort(home_table(key)).astype(jnp.int32)
    chosen = inverse[picked * BANK_DEV + within]
    return chosen.reshape(N_BANK, N_BLK * NCH_DEV, NEIGH).astype(jnp.int32)


def block_levels(key, dims, shards, least, high):
    def one(dim, blocks):
        steps = jax.random.uniform(jax.random.fold_in(jax.random.fold_in(key, 6), dim), (blocks,), jnp.float32, least / len(shards), high / len(shards))
        return jnp.repeat(jnp.exp(steps), dims[dim] // blocks).reshape((-1,) + (1,) * (len(dims) - dim - 1))

    loudness = one(*shards[0])
    for cut in shards[1:]:
        loudness = loudness * one(*cut)
    return loudness


def gaussian(rng, shape, scale, most, shards=(), held_as=jnp.bfloat16):
    loudness = block_levels(rng, shape, shards, -0.22, 0.18) if shards else 1.0
    result = jax.random.normal(rng, shape, jnp.float32) * scale * loudness
    return jnp.minimum(jnp.maximum(result, -most), most).astype(held_as)


def setup_inputs(seed: int = 0) -> dict:
    key_list = jax.random.split(jax.random.key(seed), 9)
    return {
        "self_queries": draw_self_queries(jax.random.fold_in(key_list[8], 71), 0),
        "cache_keys": draw_cache_keys(jax.random.fold_in(key_list[8], 71), 0),
        "cache_values": gaussian(key_list[2], (N_BANK, SESSION, KVW), 1.0, 6.0, ((0, 8), (1, 4))),
        "cache_lengths": draw_cache_lengths(jax.random.fold_in(key_list[8], 71), 0),
        "cross_queries": draw_cross_queries(jax.random.fold_in(key_list[8], 71), 0),
        "bank_kv": draw_bank_kv(jax.random.fold_in(key_list[8], 71), 0),
        "span_home": draw_span_home(jax.random.fold_in(key_list[8], 71), 0),
        "neighbours": draw_neighbours(jax.random.fold_in(key_list[8], 71), 0),
    }


def partial_attention(queries, keys, values, valid):
    rows = queries.shape[0]
    width = keys.shape[0]
    query_heads = queries.astype(jnp.float32).reshape(rows, HEADS, HD)
    key_heads = keys.astype(jnp.float32).reshape(width, HEADS, HD)
    value_heads = values.astype(jnp.float32).reshape(width, HEADS, HD)
    scores = jnp.einsum("rhd,chd->hrc", query_heads, key_heads) * (HD ** -0.5)
    scores = jnp.where(valid[None, None, :], scores, -jnp.inf)
    top = jnp.max(scores, axis=2)
    expo = jnp.exp(scores - top[:, :, None])
    total = jnp.sum(expo, axis=2)
    weights = lax.optimization_barrier(expo.astype(jnp.bfloat16)).astype(jnp.float32)
    summed = jnp.einsum("hrc,chd->rhd", weights, value_heads)
    return summed, top.T, total.T


def session_group(items):
    queries, keys, values, lengths = items
    key_shards = keys.reshape(N_BLK, CACHE_DEV, KVW)
    value_shards = values.reshape(N_BLK, CACHE_DEV, KVW)

    def one_shard(parts):
        shard_keys, shard_values, filled = parts
        valid = jnp.arange(CACHE_DEV, dtype=jnp.int32) < filled
        return partial_attention(queries, shard_keys, shard_values, valid)

    summed, top, total = lax.map(one_shard, (key_shards, value_shards, lengths))
    best = jnp.max(top, axis=0)
    factor = jnp.exp(top - best[None])
    numer = jnp.sum(summed * factor[..., None], axis=0)
    denom = jnp.sum(total * factor, axis=0)
    return (numer / denom[..., None]).reshape(QROWS, KVW).astype(jnp.bfloat16)


def reference(self_queries, cache_keys, cache_values, cache_lengths, cross_queries, bank_kv, span_home, neighbours):
    context_out = lax.map(session_group, (self_queries, cache_keys, cache_values, cache_lengths))
    bank_keys = bank_kv[:, :, :KVW]
    bank_values = bank_kv[:, :, KVW:]
    homes = jnp.take(span_home, neighbours.reshape(N_BANK * QCH, NEIGH).astype(jnp.int32)).astype(jnp.int32)
    query_spans = cross_queries.reshape(N_BANK * QCH, SPAN, KVW)
    every_key = jnp.ones((NROW,), dtype=bool)

    def one_span(items):
        span_rows, rows_home = items

        def one_neighbour(where):
            summed, top, total = partial_attention(span_rows, bank_keys[where], bank_values[where], every_key)
            normal = lax.optimization_barrier((summed / total[..., None]).astype(jnp.bfloat16)).astype(jnp.float32)
            return normal, top, total

        normal, top, total = lax.map(one_neighbour, rows_home)
        best = jnp.max(top, axis=0)
        weight = jnp.exp(top - best[None]) * total
        numer = jnp.sum(weight[..., None] * normal, axis=0)
        denom = jnp.sum(weight, axis=0)
        return (numer / denom[..., None]).reshape(SPAN, KVW).astype(jnp.bfloat16)

    retrieved_out = lax.map(one_span, (query_spans, homes)).reshape(N_BANK, QROWS, KVW)
    return context_out, retrieved_out
```

```python
import jax
import jax.numpy as jnp
from jax import lax
from jax.experimental import pallas as pl
from jax.experimental.pallas import tpu as pltpu
from jax.sharding import PartitionSpec as P

HEADS = 8
HD = 128
SPAN = 16
NROW = 64
NEIGH = 2
TAIL = 8
LOG2E = 1.4426950408889634
LN2 = 0.6931471805599453
FAR = -1e30


def passed_along(block, axis, distance):
    devices = range(lax.axis_size(axis))
    route = [((i - distance) % len(devices), i) for i in devices]
    return lax.ppermute(block, axis, route)


def partial_scores(queries, keys, values, valid):
    rows = queries.shape[0]
    width = keys.shape[0]
    query_heads = queries.reshape(rows, HEADS, HD)
    key_heads = keys.reshape(width, HEADS, HD)
    value_heads = values.reshape(width, HEADS, HD)
    scores = jnp.einsum(
        "rhd,chd->hrc", query_heads, key_heads, preferred_element_type=jnp.float32
    ) * HD ** (-0.5)
    scores = jnp.where(valid, scores, -jnp.inf)
    top = jnp.max(scores, axis=2)
    expo = jnp.exp(scores - top[:, :, None])
    total = jnp.sum(expo, axis=2)
    weights = expo.astype(jnp.bfloat16)
    summed = jnp.einsum("hrc,chd->rhd", weights, value_heads, preferred_element_type=jnp.float32)
    return (summed, top.T, total.T)


def merge_state(state, part):
    best = jnp.maximum(state[1], part[1])
    older = jnp.exp(state[1] - best)
    newer = jnp.exp(part[1] - best)
    summed = state[0] * older[..., None] + part[0] * newer[..., None]
    return (summed, best, state[2] * older + part[2] * newer)


def cycle_pass(queries, keys, values, valid, move_queries, move_state):
    rows = queries.shape[0]
    state = (
        jnp.zeros((rows, HEADS, HD), jnp.float32),
        jnp.full((rows, HEADS), -jnp.inf, jnp.float32),
        jnp.zeros((rows, HEADS), jnp.float32),
    )

    def turn(step, carry):
        current, acc = carry
        acc = move_state(merge_state(acc, partial_scores(current, keys, values, valid)))
        return (move_queries(current), acc)

    current, state = lax.fori_loop(0, lax.axis_size("blk") - 1, turn, (queries, state))
    return move_state(merge_state(state, partial_scores(current, keys, values, valid)))


def session_attention(queries, keys, values, valid):
    rows = queries.shape[0]

    def ahead_queries(block):
        return passed_along(block, "blk", 1)

    def ahead_state(state):
        return passed_along(state, "blk", 1)

    state = cycle_pass(queries, keys, values, valid, ahead_queries, ahead_state)
    output = state[0] / state[2][..., None]
    return output.reshape(rows, HEADS * HD).astype(jnp.bfloat16)


def fetch_neighbours(cross, bank_kv, span_home, neighbours):
    spans = neighbours.shape[0]
    width = cross.shape[1]
    wanted = neighbours.reshape(-1)
    requests = wanted.shape[0]
    owners = lax.axis_size("bank")
    capacity = max(2, (requests + owners - 1) // owners)
    places = owners * capacity
    local_spans = bank_kv.shape[0]
    homes = jnp.take(span_home, wanted)
    owner = homes // local_spans
    local_slot = homes % local_spans
    hits = (owner[:, None] == jnp.arange(owners, dtype=jnp.int32)[None, :]).astype(jnp.int32)
    earlier = (jnp.arange(requests)[:, None] > jnp.arange(requests)[None, :]).astype(jnp.int32)
    rank = jnp.sum(jnp.dot(earlier, hits) * hits, axis=1)
    target = owner * capacity + rank
    placing = target[:, None] == jnp.arange(places, dtype=jnp.int32)[None, :]
    per_request = jnp.repeat(cross.reshape(spans, SPAN, width), NEIGH, axis=0)
    outgoing = jnp.einsum(
        "rs,rck->sck", placing.astype(jnp.bfloat16), per_request, preferred_element_type=jnp.float32
    ).astype(jnp.bfloat16)
    marks = jnp.sum(jnp.where(placing, local_slot[:, None], 0), axis=0).astype(jnp.bfloat16)
    outgoing = outgoing.reshape(owners, capacity, SPAN, width)
    marks = marks.reshape(owners, capacity)
    arrived, arrived_marks = (
        lax.all_to_all(outgoing, "bank", split_axis=0, concat_axis=0, tiled=True),
        lax.all_to_all(marks, "bank", split_axis=0, concat_axis=0, tiled=True),
    )
    flat_rows = arrived.reshape(owners * capacity * SPAN, width)
    row_marks = jnp.repeat(arrived_marks.reshape(-1).astype(jnp.int32), SPAN)
    bank_keys = bank_kv[:, :, :width].reshape(local_spans * NROW, width)
    bank_values = bank_kv[:, :, width:].reshape(local_spans * NROW, width)
    column_span = jnp.arange(local_spans * NROW, dtype=jnp.int32) // NROW
    valid = (row_marks[:, None] == column_span[None, :])[None]
    summed, top, total = partial_scores(flat_rows, bank_keys, bank_values, valid)
    normal = (summed / total[..., None]).astype(jnp.bfloat16).reshape(owners, capacity, SPAN, width)
    top = top.reshape(owners, capacity, SPAN, HEADS)
    total = total.reshape(owners, capacity, SPAN, HEADS)
    normal = lax.all_to_all(normal, "bank", split_axis=0, concat_axis=0, tiled=True)
    top, total = (
        lax.all_to_all(top, "bank", split_axis=0, concat_axis=0, tiled=True),
        lax.all_to_all(total, "bank", split_axis=0, concat_axis=0, tiled=True),
    )
    normal = jnp.take(normal.reshape(places, SPAN, width), target, axis=0)
    normal = normal.reshape(spans, NEIGH, SPAN, HEADS, HD).astype(jnp.float32)
    top = jnp.take(top.reshape(places, SPAN, HEADS), target, axis=0).reshape(
        spans, NEIGH, SPAN, HEADS
    )
    total = jnp.take(total.reshape(places, SPAN, HEADS), target, axis=0).reshape(
        spans, NEIGH, SPAN, HEADS
    )
    best = jnp.max(top, axis=1)
    weight = jnp.exp(top - best[:, None]) * total
    numer = jnp.sum(weight[..., None] * normal, axis=1)
    denom = jnp.sum(weight, axis=1)
    output = numer / denom[..., None]
    return output.reshape(spans * SPAN, width).astype(jnp.bfloat16)


def put_logs(out_ref, logs):
    rows = logs.shape[0]
    lanes = pl.cdiv(rows, 128) * 128
    padded = jnp.concatenate((logs, jnp.zeros((lanes - rows, 128), jnp.float32)), axis=0)
    rest = jnp.transpose(padded)[:TAIL]
    for place in range(3):
        piece = rest.astype(jnp.bfloat16)
        out_ref[rows : rows + TAIL, place * lanes : (place + 1) * lanes] = piece
        rest = rest - piece.astype(jnp.float32)


def get_logs(part_ref):
    rows = part_ref.shape[0] - TAIL
    lanes = pl.cdiv(rows, 128) * 128
    pieces = [
        part_ref[rows : rows + TAIL, place * lanes : (place + 1) * lanes].astype(jnp.float32)
        for place in range(3)
    ]
    whole = (pieces[2] + pieces[1]) + pieces[0]
    padded = jnp.concatenate((whole, jnp.zeros((128 - TAIL, lanes), jnp.float32)), axis=0)
    return jnp.transpose(padded)[:rows]


def head_columns(head):
    return slice(head * HD, (head + 1) * HD)


def attend(query_ref, key_ref, value_ref, filled, put):
    rows = query_ref.shape[0]
    width = key_ref.shape[0]
    position = lax.broadcasted_iota(jnp.int32, (1, width), 1)
    hidden = jnp.where(position < filled, 0.0, FAR)
    lane = lax.broadcasted_iota(jnp.int32, (rows, 128), 1)
    tops = jnp.zeros((rows, 128), jnp.float32)
    totals = jnp.ones((rows, 128), jnp.float32)
    for head in range(HEADS):
        columns = head_columns(head)
        scores = lax.dot_general(
            query_ref[:, columns],
            key_ref[:, columns],
            (((1,), (1,)), ((), ())),
            preferred_element_type=jnp.float32,
        )
        scores = scores * (HD ** (-0.5) * LOG2E) + hidden
        top = jnp.max(scores, axis=1, keepdims=True)
        expo = jnp.exp2(scores - top)
        total = jnp.sum(expo, axis=1, keepdims=True)
        summed = jnp.dot(
            expo.astype(jnp.bfloat16), value_ref[:, columns], preferred_element_type=jnp.float32
        )
        put(head, summed * (1.0 / total))
        tops = jnp.where(lane == head, top, tops)
        totals = jnp.where(lane == head, total, totals)
    return tops + jnp.log(totals) * LOG2E


def attend_packed(query_ref, key_ref, value_ref, filled, out_ref):
    rows = query_ref.shape[0]

    def put(head, normal):
        out_ref[:rows, head_columns(head)] = normal.astype(jnp.bfloat16)

    put_logs(out_ref, attend(query_ref, key_ref, value_ref, filled, put))


def merge_packed(first_ref, second_ref, out_ref):
    rows = first_ref.shape[0] - TAIL
    first = get_logs(first_ref)
    second = get_logs(second_ref)
    best = jnp.maximum(first, second)
    first = jnp.exp2(first - best)
    second = jnp.exp2(second - best)
    total = first + second
    put_logs(out_ref, best + jnp.log(total) * LOG2E)
    inverse = 1.0 / total
    first = first * inverse
    second = second * inverse
    for head in range(HEADS):
        columns = head_columns(head)
        one = slice(head, head + 1)
        out_ref[:rows, columns] = (
            first_ref[:rows, columns].astype(jnp.float32) * first[:, one]
            + second_ref[:rows, columns].astype(jnp.float32) * second[:, one]
        ).astype(jnp.bfloat16)


def is_outer():
    place = lax.axis_index("blk")
    return (place == 0) | (place == lax.axis_size("blk") - 1)


def every_kernel(filled_ref, query_ref, key_ref, value_ref, out_ref):
    attend_packed(query_ref, key_ref, value_ref, filled_ref[0, 0], out_ref)


def outer_kernel(filled_ref, query_ref, key_ref, value_ref, out_ref):
    @pl.when(is_outer())
    def _():
        attend_packed(query_ref, key_ref, value_ref, filled_ref[0, 0], out_ref)


def inner_kernel(filled_ref, query_ref, key_ref, value_ref, out_ref):
    @pl.when(jnp.logical_not(is_outer()))
    def _():
        attend_packed(query_ref, key_ref, value_ref, filled_ref[0, 0], out_ref)


def turning_kernel(filled_ref, outer_ref, inner_ref, other_ref, key_ref, value_ref, out_ref, own_ref):
    @pl.when(is_outer())
    def _():
        attend_packed(outer_ref, key_ref, value_ref, filled_ref[0, 0], out_ref)

    @pl.when(jnp.logical_not(is_outer()))
    def _():
        attend_packed(inner_ref, key_ref, value_ref, filled_ref[0, 0], own_ref)
        merge_packed(own_ref, other_ref, out_ref)


def joining_kernel(own_a_ref, other_a_ref, own_b_ref, other_b_ref, out_a_ref, out_b_ref):
    @pl.when(jnp.logical_not(is_outer()))
    def _():
        merge_packed(own_a_ref, other_a_ref, out_a_ref)
        merge_packed(own_b_ref, other_b_ref, out_b_ref)


def closing_kernel(own_ref, outer_ref, inner_a_ref, inner_b_ref, out_ref):
    rows = out_ref.shape[0]

    def close(refs):
        logs = [get_logs(ref) for ref in refs]
        best = logs[0]
        for log in logs[1:]:
            best = jnp.maximum(best, log)
        factors = [jnp.exp2(log - best) for log in logs]
        inverse = 1.0 / sum(factors[1:], factors[0])
        factors = [factor * inverse for factor in factors]
        for head in range(HEADS):
            columns = head_columns(head)
            one = slice(head, head + 1)
            terms = [
                ref[:rows, columns].astype(jnp.float32) * factor[:, one]
                for ref, factor in zip(refs, factors)
            ]
            out_ref[:, columns] = sum(terms[1:], terms[0]).astype(jnp.bfloat16)

    @pl.when(is_outer())
    def _():
        close((own_ref, outer_ref))

    @pl.when(jnp.logical_not(is_outer()))
    def _():
        close((own_ref, inner_a_ref, inner_b_ref))


def spans_kernel(home_ref, wanted_ref, cross_ref, *refs):
    sources = refs[:8]
    out_ref, bank_ref, arrivals = refs[8:]
    spans = wanted_ref.shape[0]
    held = bank_ref.shape[1]
    width = cross_ref.shape[1]
    copies = [
        pltpu.make_async_copy(source, bank_ref.at[place], arrivals.at[place])
        for place, source in enumerate(sources)
    ]
    for copy in copies:
        copy.start()
    for copy in copies:
        copy.wait()
    here = lax.axis_index("bank")
    row_head = lax.broadcasted_iota(jnp.int32, (HEADS * SPAN, width), 0) // SPAN
    column_head = lax.broadcasted_iota(jnp.int32, (HEADS * SPAN, width), 1) // HD
    mine = row_head == column_head

    def one_span(span, carry):
        start = pl.multiple_of(span * SPAN, SPAN)
        query = cross_ref[pl.ds(start, SPAN), :]
        spread = jnp.concatenate([query] * HEADS, axis=0)
        spread = jnp.where(mine, spread, jnp.zeros_like(spread))
        pairs = []
        for which in range(NEIGH):
            home = home_ref[wanted_ref[span, which]]
            owner = home // held
            pairs.append((owner ^ here, home - owner * held))
        keys = jnp.concatenate([bank_ref[place, slot, :, :width] for place, slot in pairs], axis=0)
        values = jnp.concatenate([bank_ref[place, slot, :, width:] for place, slot in pairs], axis=0)
        scores = lax.dot_general(
            spread, keys, (((1,), (1,)), ((), ())), preferred_element_type=jnp.float32
        ) * (HD ** (-0.5) * LOG2E)
        top = jnp.max(scores, axis=1, keepdims=True)
        expo = jnp.exp2(scores - top)
        total = jnp.sum(expo, axis=1, keepdims=True)
        weights = (expo * (1.0 / total)).astype(jnp.bfloat16)
        for head in range(HEADS):
            columns = head_columns(head)
            out_ref[pl.ds(start, SPAN), columns] = jnp.dot(
                weights[head * SPAN : (head + 1) * SPAN],
                values[:, columns],
                preferred_element_type=jnp.float32,
            ).astype(jnp.bfloat16)
        return carry

    lax.fori_loop(0, spans, one_span, 0)


SMALL = pl.BlockSpec(memory_space=pltpu.SMEM)
WHOLE = pl.BlockSpec(memory_space=pltpu.VMEM)
AWAY = pl.BlockSpec(memory_space=pl.ANY)


def on_core(kernel, shapes, in_specs, scratch=(), flops=0, moved=0, name=None):
    return pl.pallas_call(
        kernel,
        out_shape=shapes,
        in_specs=in_specs,
        out_specs=jax.tree.map(lambda _: WHOLE, shapes),
        scratch_shapes=scratch,
        cost_estimate=pl.CostEstimate(flops=flops, transcendentals=0, bytes_accessed=moved),
        compiler_params=pltpu.CompilerParams(vmem_limit_bytes=40 << 20),
        name=name,
    )


def after(block, *others):
    return lax.optimization_barrier((block, *others))[0]


def joint_pass(queries, keys, values, filled, cross, bank_kv, span_home, wanted):
    rows, width = queries.shape
    length = keys.shape[0]
    packed = jax.ShapeDtypeStruct((rows + TAIL, width), jnp.bfloat16)
    plain = jax.ShapeDtypeStruct((rows, width), jnp.bfloat16)
    flops = 4 * rows * length * width
    moved = 4 * (rows + length) * width

    def over_blk(block, *route):
        return lax.ppermute(block, "blk", route)

    def over_bank(block, distance):
        route = [(i, i ^ distance) for i in range(lax.axis_size("bank"))]
        return lax.ppermute(block, "bank", route)

    def attention(kernel, name, block):
        call = on_core(kernel, packed, [SMALL] + [WHOLE] * 3, flops=flops, moved=moved, name=name)
        return call(filled, block, keys, values)

    far = over_blk(queries, (0, 3), (3, 0))
    bank_x = over_bank(bank_kv, 2)
    bank_y = over_bank(bank_kv, 4)
    bank_xy = over_bank(bank_kv, 6)
    bank_c = over_bank(bank_kv, 1)
    own = attention(every_kernel, "own", queries)
    near_queries = after(queries, own)
    side = over_blk(near_queries, (0, 1), (1, 0), (2, 3), (3, 2))
    middle = over_blk(near_queries, (1, 2), (2, 1))
    far_part = attention(outer_kernel, "far", far)
    far_sent = over_blk(far_part, (0, 1), (3, 2))
    passed_out = over_blk(middle, (1, 0), (2, 3))
    passed_in = over_blk(side, (1, 2), (2, 1))
    side_part = attention(every_kernel, "side", side)
    middle_part = attention(inner_kernel, "middle", middle)
    turned = on_core(
        turning_kernel,
        packed,
        [SMALL] + [WHOLE] * 5,
        scratch=(pltpu.VMEM(packed.shape, packed.dtype),),
        flops=flops,
        moved=moved,
        name="turning",
    )(filled, passed_out, passed_in, far_sent, keys, values)
    turned_out = over_blk(turned, (0, 1), (3, 2))
    turned_in = over_blk(turned, (1, 2), (2, 1))
    side_sent = over_blk(after(side_part, turned), (0, 1), (3, 2))
    middle_joined, side_joined = on_core(
        joining_kernel, (packed, packed), [WHOLE] * 4, flops=8 * rows * width, moved=16 * rows * width, name="joining"
    )(middle_part, turned_out, side_part, turned_in)
    middle_sent = over_blk(middle_joined, (1, 2), (2, 1))
    outer_sent = over_blk(side_joined, (1, 0), (2, 3))
    context = on_core(
        closing_kernel, plain, [WHOLE] * 4, flops=8 * rows * width, moved=10 * rows * width, name="closing"
    )(own, outer_sent, side_sent, middle_sent)

    banks = [bank_kv, bank_c, bank_x, over_bank(bank_x, 1)]
    banks += [bank_y, over_bank(bank_y, 1), bank_xy, over_bank(bank_xy, 1)]
    retrieved = on_core(
        spans_kernel,
        plain,
        [SMALL, SMALL, WHOLE] + [AWAY] * 8,
        scratch=(pltpu.VMEM((8, *bank_kv.shape), bank_kv.dtype), pltpu.SemaphoreType.DMA((8,))),
        flops=8 * rows * NEIGH * NROW * width,
        moved=20 * bank_kv.size,
        name="spans",
    )(span_home, wanted, cross, *banks)
    return context, retrieved


def on_device(
    self_queries,
    cache_keys,
    cache_values,
    cache_lengths,
    cross_queries,
    bank_kv,
    span_home,
    neighbours,
):
    queries = self_queries[0]
    keys = cache_keys[0]
    values = cache_values[0]
    valid = (jnp.arange(keys.shape[0], dtype=jnp.int32) < cache_lengths[0, 0])[None, None, :]
    if lax.axis_size("blk") == 4 and lax.axis_size("bank") == 8:
        context, retrieved = joint_pass(
            queries, keys, values, cache_lengths, cross_queries[0], bank_kv, span_home, neighbours[0]
        )
        return (context[None], retrieved[None])
    context = session_attention(queries, keys, values, valid)
    retrieved = fetch_neighbours(cross_queries[0], bank_kv, span_home, neighbours[0])
    return (context[None], retrieved[None])


def solution(mesh):
    return jax.shard_map(
        on_device,
        mesh=mesh,
        in_specs=(
            P("bank", "blk", None),
            P("bank", "blk", None),
            P("bank", "blk", None),
            P("bank", "blk"),
            P("bank", "blk", None),
            P("bank", None, None),
            P(),
            P("bank", "blk", None),
        ),
        out_specs=(P("bank", "blk", None), P("bank", "blk", None)),
        check_vma=False,
    )
```

```python
import functools

import jax
import jax.numpy as jnp
from jax import lax
from jax.experimental import pallas as pl
from jax.experimental.pallas import tpu as pltpu
from jax.sharding import PartitionSpec as P

HEADS = 8
HD = 128
SPAN = 16
NROW = 64
NEIGH = 2
TAIL = 8
LOG2E = 1.4426950408889634
LN2 = 0.6931471805599453
FAR = -1e30


def passed_along(block, axis, distance):
    devices = range(lax.axis_size(axis))
    route = [((i - distance) % len(devices), i) for i in devices]
    return lax.ppermute(block, axis, route)


def partial_scores(queries, keys, values, valid):
    rows = queries.shape[0]
    width = keys.shape[0]
    query_heads = queries.reshape(rows, HEADS, HD)
    key_heads = keys.reshape(width, HEADS, HD)
    value_heads = values.reshape(width, HEADS, HD)
    scores = jnp.einsum(
        "rhd,chd->hrc", query_heads, key_heads, preferred_element_type=jnp.float32
    ) * HD ** (-0.5)
    scores = jnp.where(valid, scores, -jnp.inf)
    top = jnp.max(scores, axis=2)
    expo = jnp.exp(scores - top[:, :, None])
    total = jnp.sum(expo, axis=2)
    weights = expo.astype(jnp.bfloat16)
    summed = jnp.einsum("hrc,chd->rhd", weights, value_heads, preferred_element_type=jnp.float32)
    return (summed, top.T, total.T)


def merge_state(state, part):
    best = jnp.maximum(state[1], part[1])
    older = jnp.exp(state[1] - best)
    newer = jnp.exp(part[1] - best)
    summed = state[0] * older[..., None] + part[0] * newer[..., None]
    return (summed, best, state[2] * older + part[2] * newer)


def cycle_pass(queries, keys, values, valid, move_queries, move_state):
    rows = queries.shape[0]
    state = (
        jnp.zeros((rows, HEADS, HD), jnp.float32),
        jnp.full((rows, HEADS), -jnp.inf, jnp.float32),
        jnp.zeros((rows, HEADS), jnp.float32),
    )

    def turn(step, carry):
        current, acc = carry
        acc = move_state(merge_state(acc, partial_scores(current, keys, values, valid)))
        return (move_queries(current), acc)

    current, state = lax.fori_loop(0, lax.axis_size("blk") - 1, turn, (queries, state))
    return move_state(merge_state(state, partial_scores(current, keys, values, valid)))


def session_attention(queries, keys, values, valid):
    rows = queries.shape[0]

    def ahead_queries(block):
        return passed_along(block, "blk", 1)

    def ahead_state(state):
        return passed_along(state, "blk", 1)

    state = cycle_pass(queries, keys, values, valid, ahead_queries, ahead_state)
    output = state[0] / state[2][..., None]
    return output.reshape(rows, HEADS * HD).astype(jnp.bfloat16)


def fetch_neighbours(cross, bank_kv, span_home, neighbours):
    spans = neighbours.shape[0]
    width = cross.shape[1]
    wanted = neighbours.reshape(-1)
    requests = wanted.shape[0]
    owners = lax.axis_size("bank")
    capacity = max(2, (requests + owners - 1) // owners)
    places = owners * capacity
    local_spans = bank_kv.shape[0]
    homes = jnp.take(span_home, wanted)
    owner = homes // local_spans
    local_slot = homes % local_spans
    hits = (owner[:, None] == jnp.arange(owners, dtype=jnp.int32)[None, :]).astype(jnp.int32)
    earlier = (jnp.arange(requests)[:, None] > jnp.arange(requests)[None, :]).astype(jnp.int32)
    rank = jnp.sum(jnp.dot(earlier, hits) * hits, axis=1)
    target = owner * capacity + rank
    placing = target[:, None] == jnp.arange(places, dtype=jnp.int32)[None, :]
    per_request = jnp.repeat(cross.reshape(spans, SPAN, width), NEIGH, axis=0)
    outgoing = jnp.einsum(
        "rs,rck->sck", placing.astype(jnp.bfloat16), per_request, preferred_element_type=jnp.float32
    ).astype(jnp.bfloat16)
    marks = jnp.sum(jnp.where(placing, local_slot[:, None], 0), axis=0).astype(jnp.bfloat16)
    outgoing = outgoing.reshape(owners, capacity, SPAN, width)
    marks = marks.reshape(owners, capacity)
    arrived, arrived_marks = (
        lax.all_to_all(outgoing, "bank", split_axis=0, concat_axis=0, tiled=True),
        lax.all_to_all(marks, "bank", split_axis=0, concat_axis=0, tiled=True),
    )
    flat_rows = arrived.reshape(owners * capacity * SPAN, width)
    row_marks = jnp.repeat(arrived_marks.reshape(-1).astype(jnp.int32), SPAN)
    bank_keys = bank_kv[:, :, :width].reshape(local_spans * NROW, width)
    bank_values = bank_kv[:, :, width:].reshape(local_spans * NROW, width)
    column_span = jnp.arange(local_spans * NROW, dtype=jnp.int32) // NROW
    valid = (row_marks[:, None] == column_span[None, :])[None]
    summed, top, total = partial_scores(flat_rows, bank_keys, bank_values, valid)
    normal = (summed / total[..., None]).astype(jnp.bfloat16).reshape(owners, capacity, SPAN, width)
    top = top.reshape(owners, capacity, SPAN, HEADS)
    total = total.reshape(owners, capacity, SPAN, HEADS)
    normal = lax.all_to_all(normal, "bank", split_axis=0, concat_axis=0, tiled=True)
    top, total = (
        lax.all_to_all(top, "bank", split_axis=0, concat_axis=0, tiled=True),
        lax.all_to_all(total, "bank", split_axis=0, concat_axis=0, tiled=True),
    )
    normal = jnp.take(normal.reshape(places, SPAN, width), target, axis=0)
    normal = normal.reshape(spans, NEIGH, SPAN, HEADS, HD).astype(jnp.float32)
    top = jnp.take(top.reshape(places, SPAN, HEADS), target, axis=0).reshape(
        spans, NEIGH, SPAN, HEADS
    )
    total = jnp.take(total.reshape(places, SPAN, HEADS), target, axis=0).reshape(
        spans, NEIGH, SPAN, HEADS
    )
    best = jnp.max(top, axis=1)
    weight = jnp.exp(top - best[:, None]) * total
    numer = jnp.sum(weight[..., None] * normal, axis=1)
    denom = jnp.sum(weight, axis=1)
    output = numer / denom[..., None]
    return output.reshape(spans * SPAN, width).astype(jnp.bfloat16)


HALF = HEADS // 2
HALF_WIDTH = HALF * HD


def put_logs(out_ref, logs):
    rows = logs.shape[0]
    lanes = pl.cdiv(rows, 128) * 128
    padded = jnp.concatenate((logs, jnp.zeros((lanes - rows, 128), jnp.float32)), axis=0)
    whole = jnp.transpose(padded)[:TAIL]
    first = whole.astype(jnp.bfloat16).astype(jnp.float32)
    rest = whole - first
    second = rest.astype(jnp.bfloat16).astype(jnp.float32)
    upper = lax.broadcasted_iota(jnp.int32, (TAIL, lanes), 0) < HALF
    out_ref[rows:, :lanes] = jnp.where(upper, first, rest - second).astype(jnp.bfloat16)
    out_ref[rows:, lanes : 2 * lanes] = second.astype(jnp.bfloat16)


def get_logs(part_ref):
    rows = part_ref.shape[0] - TAIL
    lanes = pl.cdiv(rows, 128) * 128
    first = part_ref[rows:, :lanes].astype(jnp.float32)
    second = part_ref[rows:, lanes : 2 * lanes].astype(jnp.float32)
    whole = (pltpu.roll(first, HALF, 0) + second) + first
    padded = jnp.concatenate((whole, jnp.zeros((128 - TAIL, lanes), jnp.float32)), axis=0)
    return jnp.transpose(padded)[:rows]


def head_columns(head):
    return slice(head * HD, (head + 1) * HD)


def attend(query_ref, key_ref, value_ref, filled_ref, half, out_ref):
    rows = query_ref.shape[0]
    width = key_ref.shape[0]
    position = lax.broadcasted_iota(jnp.int32, (1, width), 1)
    hidden = jnp.where(position < filled_ref[0, 0], 0.0, FAR)
    lane = lax.broadcasted_iota(jnp.int32, (rows, 128), 1)
    tops = jnp.zeros((rows, 128), jnp.float32)
    totals = jnp.ones((rows, 128), jnp.float32)
    for place in range(HALF):
        columns = head_columns(half * HALF + place)
        scores = lax.dot_general(
            query_ref[:, columns],
            key_ref[:, columns],
            (((1,), (1,)), ((), ())),
            preferred_element_type=jnp.float32,
        )
        scores = scores * (HD ** (-0.5) * LOG2E) + hidden
        top = jnp.max(scores, axis=1, keepdims=True)
        expo = jnp.exp2(scores - top)
        total = jnp.sum(expo, axis=1, keepdims=True)
        summed = jnp.dot(
            expo.astype(jnp.bfloat16), value_ref[:, columns], preferred_element_type=jnp.float32
        )
        out_ref[:rows, head_columns(place)] = (summed * (1.0 / total)).astype(jnp.bfloat16)
        chosen = (lane == place) | (lane == place + HALF)
        tops = jnp.where(chosen, top, tops)
        totals = jnp.where(chosen, total, totals)
    put_logs(out_ref, tops + jnp.log(totals) * LOG2E)


def merge(refs, out_ref, columns, log_ref=None):
    rows = refs[0].shape[0] - TAIL
    logs = [get_logs(ref) for ref in refs]
    best = logs[0]
    for log in logs[1:]:
        best = jnp.maximum(best, log)
    factors = [jnp.exp2(log - best) for log in logs]
    total = sum(factors[1:], factors[0])
    if log_ref is not None:
        put_logs(log_ref, best + jnp.log(total) * LOG2E)
    inverse = 1.0 / total
    factors = [factor * inverse for factor in factors]
    for place in range(HALF):
        terms = [
            ref[:rows, head_columns(place)].astype(jnp.float32) * factor[:, place : place + 1]
            for ref, factor in zip(refs, factors)
        ]
        joined = sum(terms[1:], terms[0]).astype(jnp.bfloat16)
        out_ref[:rows, slice(columns + place * HD, columns + (place + 1) * HD)] = joined


def is_outer():
    place = lax.axis_index("blk")
    return (place == 0) | (place == lax.axis_size("blk") - 1)


def when_outer(body):
    pl.when(is_outer())(body)


def when_inner(body):
    pl.when(jnp.logical_not(is_outer()))(body)


def whole_kernel(filled_ref, query_ref, key_ref, value_ref, out_ref):
    for half in range(2):
        attend(query_ref, key_ref, value_ref, filled_ref, half, out_ref.at[half])


def outer_kernel(*refs):
    @when_outer
    def _():
        whole_kernel(*refs)


def inner_kernel(*refs):
    @when_inner
    def _():
        whole_kernel(*refs)


def passed_kernel(filled_ref, query_ref, key_ref, value_ref, other_ref, out_ref, own_ref):
    @when_inner
    def _():
        for half in range(2):
            attend(query_ref, key_ref, value_ref, filled_ref, half, own_ref)
            merge((own_ref, other_ref.at[half]), out_ref.at[half], 0, out_ref.at[half])


def join_kernel(middle_ref, outer_ref, side_ref, inner_ref, to_middle_ref, to_side_ref):
    @when_outer
    def _():
        to_side_ref[...] = side_ref[...]

    @when_inner
    def _():
        for half in range(2):
            to_middle, to_side = to_middle_ref.at[half], to_side_ref.at[half]
            merge((middle_ref.at[half], outer_ref.at[half]), to_middle, 0, to_middle)
            merge((side_ref.at[half], inner_ref.at[half]), to_side, 0, to_side)


def closing_kernel(own_ref, side_ref, middle_ref, out_ref):
    @when_outer
    def _():
        for half in range(2):
            merge((own_ref.at[half], side_ref.at[half]), out_ref, half * HALF_WIDTH)

    @when_inner
    def _():
        for half in range(2):
            parts = (own_ref.at[half], side_ref.at[half], middle_ref.at[half])
            merge(parts, out_ref, half * HALF_WIDTH)


def spans_kernel(home_ref, wanted_ref, cross_ref, *refs):
    own_ref, core_ref, others_ref, core_others_ref, out_ref, bank_ref, arrivals = refs
    sources = [own_ref, core_ref]
    for place in range(3):
        sources += [others_ref.at[place], core_others_ref.at[place]]
    spans = wanted_ref.shape[1]
    held = bank_ref.shape[1]
    width = cross_ref.shape[1]
    copies = [
        pltpu.make_async_copy(source, bank_ref.at[place], arrivals.at[place])
        for place, source in enumerate(sources)
    ]
    for copy in copies:
        copy.start()
    for copy in copies:
        copy.wait()
    here = lax.axis_index("bank")
    row_head = lax.broadcasted_iota(jnp.int32, (HEADS * SPAN, width), 0) // SPAN
    column_head = lax.broadcasted_iota(jnp.int32, (HEADS * SPAN, width), 1) // HD
    mine = row_head == column_head

    def one_span(span, carry):
        start = pl.multiple_of(span * SPAN, SPAN)
        query = cross_ref[pl.ds(start, SPAN), :]
        spread = jnp.concatenate([query] * HEADS, axis=0)
        spread = jnp.where(mine, spread, jnp.zeros_like(spread))
        pairs = []
        for which in range(NEIGH):
            home = home_ref[wanted_ref[which, span]]
            owner = home // held
            pairs.append((owner ^ here, home - owner * held))
        keys = jnp.concatenate([bank_ref[place, slot, :, :width] for place, slot in pairs], axis=0)
        values = jnp.concatenate([bank_ref[place, slot, :, width:] for place, slot in pairs], axis=0)
        scores = lax.dot_general(
            spread, keys, (((1,), (1,)), ((), ())), preferred_element_type=jnp.float32
        ) * (HD ** (-0.5) * LOG2E)
        top = jnp.max(scores, axis=1, keepdims=True)
        expo = jnp.exp2(scores - top)
        total = jnp.sum(expo, axis=1, keepdims=True)
        weights = (expo * (1.0 / total)).astype(jnp.bfloat16)
        for head in range(HEADS):
            columns = head_columns(head)
            out_ref[pl.ds(start, SPAN), columns] = jnp.dot(
                weights[head * SPAN : (head + 1) * SPAN],
                values[:, columns],
                preferred_element_type=jnp.float32,
            ).astype(jnp.bfloat16)
        return carry

    lax.fori_loop(0, spans, one_span, 0, unroll=True)


SMALL = pl.BlockSpec(memory_space=pltpu.SMEM)
WHOLE = pl.BlockSpec(memory_space=pltpu.VMEM)
AWAY = pl.BlockSpec(memory_space=pl.ANY)


def on_core(kernel, shapes, in_specs, scratch=(), name=None):
    return pl.pallas_call(
        kernel,
        out_shape=shapes,
        in_specs=in_specs,
        out_specs=jax.tree.map(lambda _: WHOLE, shapes),
        scratch_shapes=scratch,
        cost_estimate=pl.CostEstimate(flops=1, transcendentals=0, bytes_accessed=1),
        compiler_params=pltpu.CompilerParams(vmem_limit_bytes=(10 if name == "spans" else 5) << 20),
        name=name,
    )


def after(block, *others):
    return lax.optimization_barrier((block, *others))[0]


def joint_pass(queries, keys, values, filled, cross, bank_kv, span_home, wanted):
    rows, width = queries.shape
    whole_part = jax.ShapeDtypeStruct((2, rows + TAIL, HALF_WIDTH), jnp.bfloat16)
    plain = jax.ShapeDtypeStruct((rows, width), jnp.bfloat16)

    def over_blk(block, *route):
        return lax.ppermute(block, "blk", route)

    def over_bank(block, distance):
        route = [(i, i ^ distance) for i in range(lax.axis_size("bank"))]
        return lax.ppermute(block, "bank", route)

    def attention(kernel, name, block):
        return on_core(kernel, whole_part, [SMALL] + [WHOLE] * 3, name=name)(filled, block, keys, values)

    swap_far = ((0, 3), (3, 0))
    swap_side = ((0, 1), (1, 0), (2, 3), (3, 2))
    swap_middle = ((1, 2), (2, 1))
    inward = ((0, 1), (3, 2))
    outward = ((1, 0), (2, 3))

    far = over_blk(queries, *swap_far)
    core_c = over_bank(bank_kv, 1)
    near = after(queries, core_c)
    side = over_blk(near, *swap_side)
    middle = over_blk(near, *swap_middle)
    near_bank = after(bank_kv, core_c)
    bank_x = over_bank(near_bank, 2)
    bank_y = over_bank(near_bank, 4)
    own = attention(whole_kernel, "own", near)
    passed_in = over_blk(side, *swap_middle)
    passed_out = over_blk(middle, *outward)
    far_part = attention(outer_kernel, "far", after(far, own, side, middle, bank_x, bank_y))
    far_sent = over_blk(far_part, *inward)
    turned = attention(outer_kernel, "turned", after(passed_out, passed_in))
    bank_xy = over_bank(after(bank_kv, far_part), 6)
    from_outer = over_blk(turned, *inward)
    met = on_core(
        passed_kernel,
        whole_part,
        [SMALL] + [WHOLE] * 4,
        scratch=(pltpu.VMEM(whole_part.shape[1:], whole_part.dtype),),
        name="passed",
    )(filled, after(passed_in, turned), keys, values, far_sent)
    from_middle = over_blk(met, *swap_middle)
    others = after(jnp.stack((bank_x, bank_y, bank_xy)), met)
    core_others = over_bank(others, 1)
    side_part = attention(whole_kernel, "side", after(side, met, from_outer))
    middle_part = attention(inner_kernel, "middle", after(middle, side_part))
    to_middle, to_side = on_core(join_kernel, (whole_part, whole_part), [WHOLE] * 4, name="join")(
        middle_part, from_outer, side_part, from_middle
    )
    home_middle = over_blk(to_middle, *swap_middle)
    home_side = over_blk(to_side, *swap_side)

    retrieved = on_core(
        spans_kernel,
        plain,
        [SMALL, SMALL, WHOLE] + [AWAY] * 4,
        scratch=(pltpu.VMEM((8, *bank_kv.shape), bank_kv.dtype), pltpu.SemaphoreType.DMA((8,))),
        name="spans",
    )(span_home, wanted.T, after(cross, to_side), bank_kv, core_c, others, core_others)
    context = on_core(closing_kernel, plain, [WHOLE] * 3, name="closing")(
        after(own, retrieved), home_side, home_middle
    )
    return context, retrieved


def on_device(
    self_queries,
    cache_keys,
    cache_values,
    cache_lengths,
    cross_queries,
    bank_kv,
    span_home,
    neighbours,
):
    queries = self_queries[0]
    keys = cache_keys[0]
    values = cache_values[0]
    valid = (jnp.arange(keys.shape[0], dtype=jnp.int32) < cache_lengths[0, 0])[None, None, :]
    if lax.axis_size("blk") == 4 and lax.axis_size("bank") == 8:
        context, retrieved = joint_pass(
            queries, keys, values, cache_lengths, cross_queries[0], bank_kv, span_home, neighbours[0]
        )
        return (context[None], retrieved[None])
    context = session_attention(queries, keys, values, valid)
    retrieved = fetch_neighbours(cross_queries[0], bank_kv, span_home, neighbours[0])
    return (context[None], retrieved[None])


def solution(mesh):
    return jax.shard_map(
        on_device,
        mesh=mesh,
        in_specs=(
            P("bank", "blk", None),
            P("bank", "blk", None),
            P("bank", "blk", None),
            P("bank", "blk"),
            P("bank", "blk", None),
            P("bank", None, None),
            P(),
            P("bank", "blk", None),
        ),
        out_specs=(P("bank", "blk", None), P("bank", "blk", None)),
        check_vma=False,
    )
```

```python
import functools

import jax
import jax.numpy as jnp
from jax import lax
from jax.experimental import pallas as pl
from jax.experimental.pallas import tpu as pltpu
from jax.sharding import PartitionSpec as P

HEADS = 8
HD = 128
SPAN = 16
NROW = 64
NEIGH = 2
TAIL = 8
LOG2E = 1.4426950408889634
LN2 = 0.6931471805599453
FAR = -1e30


def passed_along(block, axis, distance):
    devices = range(lax.axis_size(axis))
    route = [((i - distance) % len(devices), i) for i in devices]
    return lax.ppermute(block, axis, route)


def partial_scores(queries, keys, values, valid):
    rows = queries.shape[0]
    width = keys.shape[0]
    query_heads = queries.reshape(rows, HEADS, HD)
    key_heads = keys.reshape(width, HEADS, HD)
    value_heads = values.reshape(width, HEADS, HD)
    scores = jnp.einsum(
        "rhd,chd->hrc", query_heads, key_heads, preferred_element_type=jnp.float32
    ) * HD ** (-0.5)
    scores = jnp.where(valid, scores, -jnp.inf)
    top = jnp.max(scores, axis=2)
    expo = jnp.exp(scores - top[:, :, None])
    total = jnp.sum(expo, axis=2)
    weights = expo.astype(jnp.bfloat16)
    summed = jnp.einsum("hrc,chd->rhd", weights, value_heads, preferred_element_type=jnp.float32)
    return (summed, top.T, total.T)


def merge_state(state, part):
    best = jnp.maximum(state[1], part[1])
    older = jnp.exp(state[1] - best)
    newer = jnp.exp(part[1] - best)
    summed = state[0] * older[..., None] + part[0] * newer[..., None]
    return (summed, best, state[2] * older + part[2] * newer)


def cycle_pass(queries, keys, values, valid, move_queries, move_state):
    rows = queries.shape[0]
    state = (
        jnp.zeros((rows, HEADS, HD), jnp.float32),
        jnp.full((rows, HEADS), -jnp.inf, jnp.float32),
        jnp.zeros((rows, HEADS), jnp.float32),
    )

    def turn(step, carry):
        current, acc = carry
        acc = move_state(merge_state(acc, partial_scores(current, keys, values, valid)))
        return (move_queries(current), acc)

    current, state = lax.fori_loop(0, lax.axis_size("blk") - 1, turn, (queries, state))
    return move_state(merge_state(state, partial_scores(current, keys, values, valid)))


def session_attention(queries, keys, values, valid):
    rows = queries.shape[0]

    def ahead_queries(block):
        return passed_along(block, "blk", 1)

    def ahead_state(state):
        return passed_along(state, "blk", 1)

    state = cycle_pass(queries, keys, values, valid, ahead_queries, ahead_state)
    output = state[0] / state[2][..., None]
    return output.reshape(rows, HEADS * HD).astype(jnp.bfloat16)


def fetch_neighbours(cross, bank_kv, span_home, neighbours):
    spans = neighbours.shape[0]
    width = cross.shape[1]
    wanted = neighbours.reshape(-1)
    requests = wanted.shape[0]
    owners = lax.axis_size("bank")
    capacity = max(2, (requests + owners - 1) // owners)
    places = owners * capacity
    local_spans = bank_kv.shape[0]
    homes = jnp.take(span_home, wanted)
    owner = homes // local_spans
    local_slot = homes % local_spans
    hits = (owner[:, None] == jnp.arange(owners, dtype=jnp.int32)[None, :]).astype(jnp.int32)
    earlier = (jnp.arange(requests)[:, None] > jnp.arange(requests)[None, :]).astype(jnp.int32)
    rank = jnp.sum(jnp.dot(earlier, hits) * hits, axis=1)
    target = owner * capacity + rank
    placing = target[:, None] == jnp.arange(places, dtype=jnp.int32)[None, :]
    per_request = jnp.repeat(cross.reshape(spans, SPAN, width), NEIGH, axis=0)
    outgoing = jnp.einsum(
        "rs,rck->sck", placing.astype(jnp.bfloat16), per_request, preferred_element_type=jnp.float32
    ).astype(jnp.bfloat16)
    marks = jnp.sum(jnp.where(placing, local_slot[:, None], 0), axis=0).astype(jnp.bfloat16)
    outgoing = outgoing.reshape(owners, capacity, SPAN, width)
    marks = marks.reshape(owners, capacity)
    arrived, arrived_marks = (
        lax.all_to_all(outgoing, "bank", split_axis=0, concat_axis=0, tiled=True),
        lax.all_to_all(marks, "bank", split_axis=0, concat_axis=0, tiled=True),
    )
    flat_rows = arrived.reshape(owners * capacity * SPAN, width)
    row_marks = jnp.repeat(arrived_marks.reshape(-1).astype(jnp.int32), SPAN)
    bank_keys = bank_kv[:, :, :width].reshape(local_spans * NROW, width)
    bank_values = bank_kv[:, :, width:].reshape(local_spans * NROW, width)
    column_span = jnp.arange(local_spans * NROW, dtype=jnp.int32) // NROW
    valid = (row_marks[:, None] == column_span[None, :])[None]
    summed, top, total = partial_scores(flat_rows, bank_keys, bank_values, valid)
    normal = (summed / total[..., None]).astype(jnp.bfloat16).reshape(owners, capacity, SPAN, width)
    top = top.reshape(owners, capacity, SPAN, HEADS)
    total = total.reshape(owners, capacity, SPAN, HEADS)
    normal = lax.all_to_all(normal, "bank", split_axis=0, concat_axis=0, tiled=True)
    top, total = (
        lax.all_to_all(top, "bank", split_axis=0, concat_axis=0, tiled=True),
        lax.all_to_all(total, "bank", split_axis=0, concat_axis=0, tiled=True),
    )
    normal = jnp.take(normal.reshape(places, SPAN, width), target, axis=0)
    normal = normal.reshape(spans, NEIGH, SPAN, HEADS, HD).astype(jnp.float32)
    top = jnp.take(top.reshape(places, SPAN, HEADS), target, axis=0).reshape(
        spans, NEIGH, SPAN, HEADS
    )
    total = jnp.take(total.reshape(places, SPAN, HEADS), target, axis=0).reshape(
        spans, NEIGH, SPAN, HEADS
    )
    best = jnp.max(top, axis=1)
    weight = jnp.exp(top - best[:, None]) * total
    numer = jnp.sum(weight[..., None] * normal, axis=1)
    denom = jnp.sum(weight, axis=1)
    output = numer / denom[..., None]
    return output.reshape(spans * SPAN, width).astype(jnp.bfloat16)


HALF = HEADS // 2
HALF_WIDTH = HALF * HD


def put_logs(out_ref, logs):
    rows = logs.shape[0]
    lanes = pl.cdiv(rows, 128) * 128
    padded = jnp.concatenate((logs, jnp.zeros((lanes - rows, 128), jnp.float32)), axis=0)
    whole = jnp.transpose(padded)[:TAIL]
    first = whole.astype(jnp.bfloat16).astype(jnp.float32)
    rest = whole - first
    second = rest.astype(jnp.bfloat16).astype(jnp.float32)
    upper = lax.broadcasted_iota(jnp.int32, (TAIL, lanes), 0) < HALF
    out_ref[rows:, :lanes] = jnp.where(upper, first, rest - second).astype(jnp.bfloat16)
    out_ref[rows:, lanes : 2 * lanes] = second.astype(jnp.bfloat16)


def get_logs(part_ref):
    rows = part_ref.shape[0] - TAIL
    lanes = pl.cdiv(rows, 128) * 128
    first = part_ref[rows:, :lanes].astype(jnp.float32)
    second = part_ref[rows:, lanes : 2 * lanes].astype(jnp.float32)
    whole = (pltpu.roll(first, HALF, 0) + second) + first
    padded = jnp.concatenate((whole, jnp.zeros((128 - TAIL, lanes), jnp.float32)), axis=0)
    return jnp.transpose(padded)[:rows]


def head_columns(head):
    return slice(head * HD, (head + 1) * HD)


def attend(query_ref, key_ref, value_ref, filled_ref, half, out_ref):
    rows = query_ref.shape[0]
    width = key_ref.shape[0]
    position = lax.broadcasted_iota(jnp.int32, (1, width), 1)
    hidden = jnp.where(position < filled_ref[0, 0], 0.0, FAR)
    lane = lax.broadcasted_iota(jnp.int32, (rows, 128), 1)
    tops = jnp.zeros((rows, 128), jnp.float32)
    totals = jnp.ones((rows, 128), jnp.float32)
    for place in range(HALF):
        columns = head_columns(half * HALF + place)
        scores = lax.dot_general(
            query_ref[:, columns],
            key_ref[:, columns],
            (((1,), (1,)), ((), ())),
            preferred_element_type=jnp.float32,
        )
        scores = scores * (HD ** (-0.5) * LOG2E) + hidden
        top = jnp.max(scores, axis=1, keepdims=True)
        expo = jnp.exp2(scores - top)
        total = jnp.sum(expo, axis=1, keepdims=True)
        summed = jnp.dot(
            expo.astype(jnp.bfloat16), value_ref[:, columns], preferred_element_type=jnp.float32
        )
        out_ref[:rows, head_columns(place)] = (summed * (1.0 / total)).astype(jnp.bfloat16)
        chosen = (lane == place) | (lane == place + HALF)
        tops = jnp.where(chosen, top, tops)
        totals = jnp.where(chosen, total, totals)
    put_logs(out_ref, tops + jnp.log(totals) * LOG2E)


def merge(refs, out_ref, columns, log_ref=None):
    rows = refs[0].shape[0] - TAIL
    logs = [get_logs(ref) for ref in refs]
    best = logs[0]
    for log in logs[1:]:
        best = jnp.maximum(best, log)
    factors = [jnp.exp2(log - best) for log in logs]
    total = sum(factors[1:], factors[0])
    if log_ref is not None:
        put_logs(log_ref, best + jnp.log(total) * LOG2E)
    inverse = 1.0 / total
    factors = [factor * inverse for factor in factors]
    for place in range(HALF):
        terms = [
            ref[:rows, head_columns(place)].astype(jnp.float32) * factor[:, place : place + 1]
            for ref, factor in zip(refs, factors)
        ]
        joined = sum(terms[1:], terms[0]).astype(jnp.bfloat16)
        out_ref[:rows, slice(columns + place * HD, columns + (place + 1) * HD)] = joined


def is_outer():
    place = lax.axis_index("blk")
    return (place == 0) | (place == lax.axis_size("blk") - 1)


def when_outer(body):
    pl.when(is_outer())(body)


def when_inner(body):
    pl.when(jnp.logical_not(is_outer()))(body)


def whole_kernel(filled_ref, query_ref, key_ref, value_ref, out_ref):
    for half in range(2):
        attend(query_ref, key_ref, value_ref, filled_ref, half, out_ref.at[half])


def outer_kernel(*refs):
    @when_outer
    def _():
        whole_kernel(*refs)


def inner_kernel(*refs):
    @when_inner
    def _():
        whole_kernel(*refs)


def meet_kernel(own_ref, other_ref, out_ref):
    @when_inner
    def _():
        for half in range(2):
            merge((own_ref.at[half], other_ref.at[half]), out_ref.at[half], 0, out_ref.at[half])


def join_kernel(middle_ref, outer_ref, side_ref, inner_ref, to_middle_ref, to_side_ref):
    @when_outer
    def _():
        to_side_ref[...] = side_ref[...]

    @when_inner
    def _():
        for half in range(2):
            to_middle, to_side = to_middle_ref.at[half], to_side_ref.at[half]
            merge((middle_ref.at[half], outer_ref.at[half]), to_middle, 0, to_middle)
            merge((side_ref.at[half], inner_ref.at[half]), to_side, 0, to_side)


def closing_kernel(own_ref, side_ref, middle_ref, out_ref):
    @when_outer
    def _():
        for half in range(2):
            merge((own_ref.at[half], side_ref.at[half]), out_ref, half * HALF_WIDTH)

    @when_inner
    def _():
        for half in range(2):
            parts = (own_ref.at[half], side_ref.at[half], middle_ref.at[half])
            merge(parts, out_ref, half * HALF_WIDTH)


def spans_kernel(home_ref, wanted_ref, cross_ref, *refs):
    own_ref, core_ref, others_ref, core_others_ref, out_ref, bank_ref, arrivals = refs
    sources = [own_ref, core_ref]
    for place in range(3):
        sources += [others_ref.at[place], core_others_ref.at[place]]
    spans = wanted_ref.shape[1]
    held = bank_ref.shape[1]
    width = cross_ref.shape[1]
    copies = [
        pltpu.make_async_copy(source, bank_ref.at[place], arrivals.at[place])
        for place, source in enumerate(sources)
    ]
    for copy in copies:
        copy.start()
    for copy in copies:
        copy.wait()
    here = lax.axis_index("bank")
    row_head = lax.broadcasted_iota(jnp.int32, (HEADS * SPAN, width), 0) // SPAN
    column_head = lax.broadcasted_iota(jnp.int32, (HEADS * SPAN, width), 1) // HD
    mine = row_head == column_head

    def one_span(span, carry):
        start = pl.multiple_of(span * SPAN, SPAN)
        query = cross_ref[pl.ds(start, SPAN), :]
        spread = jnp.concatenate([query] * HEADS, axis=0)
        spread = jnp.where(mine, spread, jnp.zeros_like(spread))
        pairs = []
        for which in range(NEIGH):
            home = home_ref[wanted_ref[which, span]]
            owner = home // held
            pairs.append((owner ^ here, home - owner * held))
        keys = jnp.concatenate([bank_ref[place, slot, :, :width] for place, slot in pairs], axis=0)
        values = jnp.concatenate([bank_ref[place, slot, :, width:] for place, slot in pairs], axis=0)
        scores = lax.dot_general(
            spread, keys, (((1,), (1,)), ((), ())), preferred_element_type=jnp.float32
        ) * (HD ** (-0.5) * LOG2E)
        top = jnp.max(scores, axis=1, keepdims=True)
        expo = jnp.exp2(scores - top)
        total = jnp.sum(expo, axis=1, keepdims=True)
        weights = (expo * (1.0 / total)).astype(jnp.bfloat16)
        for head in range(HEADS):
            columns = head_columns(head)
            out_ref[pl.ds(start, SPAN), columns] = jnp.dot(
                weights[head * SPAN : (head + 1) * SPAN],
                values[:, columns],
                preferred_element_type=jnp.float32,
            ).astype(jnp.bfloat16)
        return carry

    lax.fori_loop(0, spans, one_span, 0, unroll=True)


SMALL = pl.BlockSpec(memory_space=pltpu.SMEM)
WHOLE = pl.BlockSpec(memory_space=pltpu.VMEM)
AWAY = pl.BlockSpec(memory_space=pl.ANY)


def on_core(kernel, shapes, in_specs, scratch=(), name=None):
    return pl.pallas_call(
        kernel,
        out_shape=shapes,
        in_specs=in_specs,
        out_specs=jax.tree.map(lambda _: WHOLE, shapes),
        scratch_shapes=scratch,
        cost_estimate=pl.CostEstimate(flops=1, transcendentals=0, bytes_accessed=1),
        compiler_params=pltpu.CompilerParams(vmem_limit_bytes=(10 if name == "spans" else 5) << 20),
        name=name,
    )


def after(block, *others):
    return lax.optimization_barrier((block, *others))[0]


def joint_pass(queries, keys, values, filled, cross, bank_kv, span_home, wanted):
    rows, width = queries.shape
    whole_part = jax.ShapeDtypeStruct((2, rows + TAIL, HALF_WIDTH), jnp.bfloat16)
    plain = jax.ShapeDtypeStruct((rows, width), jnp.bfloat16)

    def over_blk(block, *route):
        return lax.ppermute(block, "blk", route)

    def over_bank(block, distance):
        route = [(i, i ^ distance) for i in range(lax.axis_size("bank"))]
        return lax.ppermute(block, "bank", route)

    def attention(kernel, name, block):
        return on_core(kernel, whole_part, [SMALL] + [WHOLE] * 3, name=name)(filled, block, keys, values)

    swap_far = ((0, 3), (3, 0))
    swap_side = ((0, 1), (1, 0), (2, 3), (3, 2))
    swap_middle = ((1, 2), (2, 1))
    inward = ((0, 1), (3, 2))
    outward = ((1, 0), (2, 3))

    far = over_blk(queries, *swap_far)
    side = over_blk(queries, *swap_side)
    middle = over_blk(queries, *swap_middle)
    own = attention(whole_kernel, "own", queries)
    far_part = attention(outer_kernel, "far", after(far, own))
    far_sent = over_blk(far_part, *inward)
    passed_in = over_blk(after(side, far_part), *swap_middle)
    passed_out = over_blk(after(middle, far_part), *outward)
    bank_x = over_bank(after(bank_kv, far_part), 2)
    bank_y = over_bank(after(bank_kv, far_part), 4)
    turned = attention(outer_kernel, "turned", after(passed_out, passed_in))
    from_outer = over_blk(turned, *inward)
    passed = attention(inner_kernel, "passed", after(passed_in, turned))
    met = on_core(meet_kernel, whole_part, [WHOLE] * 2, name="met")(passed, far_sent)
    from_middle = over_blk(met, *swap_middle)
    side_part = attention(whole_kernel, "side", after(side, met))
    middle_part = attention(inner_kernel, "middle", after(middle, side_part))
    bank_xy = over_bank(after(bank_kv, met, bank_x, bank_y), 6)
    core_c = over_bank(after(bank_kv, met), 1)
    to_middle, to_side = on_core(join_kernel, (whole_part, whole_part), [WHOLE] * 4, name="join")(
        middle_part, from_outer, side_part, from_middle
    )
    home_middle = over_blk(to_middle, *swap_middle)
    home_side = over_blk(to_side, *swap_side)
    others = after(jnp.stack((bank_x, bank_y, bank_xy)), to_side)
    core_others = over_bank(others, 1)

    retrieved = on_core(
        spans_kernel,
        plain,
        [SMALL, SMALL, WHOLE] + [AWAY] * 4,
        scratch=(pltpu.VMEM((8, *bank_kv.shape), bank_kv.dtype), pltpu.SemaphoreType.DMA((8,))),
        name="spans",
    )(span_home, wanted.T, after(cross, to_side), bank_kv, core_c, others, core_others)
    context = on_core(closing_kernel, plain, [WHOLE] * 3, name="closing")(
        after(own, retrieved), home_side, home_middle
    )
    return context, retrieved


def on_device(
    self_queries,
    cache_keys,
    cache_values,
    cache_lengths,
    cross_queries,
    bank_kv,
    span_home,
    neighbours,
):
    queries = self_queries[0]
    keys = cache_keys[0]
    values = cache_values[0]
    valid = (jnp.arange(keys.shape[0], dtype=jnp.int32) < cache_lengths[0, 0])[None, None, :]
    if lax.axis_size("blk") == 4 and lax.axis_size("bank") == 8:
        context, retrieved = joint_pass(
            queries, keys, values, cache_lengths, cross_queries[0], bank_kv, span_home, neighbours[0]
        )
        return (context[None], retrieved[None])
    context = session_attention(queries, keys, values, valid)
    retrieved = fetch_neighbours(cross_queries[0], bank_kv, span_home, neighbours[0])
    return (context[None], retrieved[None])


def solution(mesh):
    return jax.shard_map(
        on_device,
        mesh=mesh,
        in_specs=(
            P("bank", "blk", None),
            P("bank", "blk", None),
            P("bank", "blk", None),
            P("bank", "blk"),
            P("bank", "blk", None),
            P("bank", None, None),
            P(),
            P("bank", "blk", None),
        ),
        out_specs=(P("bank", "blk", None), P("bank", "blk", None)),
        check_vma=False,
    )
```

```python
import functools

import jax
import jax.numpy as jnp
from jax import lax
from jax.experimental import pallas as pl
from jax.experimental.pallas import tpu as pltpu
from jax.sharding import PartitionSpec as P

HEADS = 8
HD = 128
SPAN = 16
NROW = 64
NEIGH = 2
TAIL = 8
LOG2E = 1.4426950408889634
LN2 = 0.6931471805599453
FAR = -1e30


def passed_along(block, axis, distance):
    devices = range(lax.axis_size(axis))
    route = [((i - distance) % len(devices), i) for i in devices]
    return lax.ppermute(block, axis, route)


def partial_scores(queries, keys, values, valid):
    rows = queries.shape[0]
    width = keys.shape[0]
    query_heads = queries.reshape(rows, HEADS, HD)
    key_heads = keys.reshape(width, HEADS, HD)
    value_heads = values.reshape(width, HEADS, HD)
    scores = jnp.einsum(
        "rhd,chd->hrc", query_heads, key_heads, preferred_element_type=jnp.float32
    ) * HD ** (-0.5)
    scores = jnp.where(valid, scores, -jnp.inf)
    top = jnp.max(scores, axis=2)
    expo = jnp.exp(scores - top[:, :, None])
    total = jnp.sum(expo, axis=2)
    weights = expo.astype(jnp.bfloat16)
    summed = jnp.einsum("hrc,chd->rhd", weights, value_heads, preferred_element_type=jnp.float32)
    return (summed, top.T, total.T)


def merge_state(state, part):
    best = jnp.maximum(state[1], part[1])
    older = jnp.exp(state[1] - best)
    newer = jnp.exp(part[1] - best)
    summed = state[0] * older[..., None] + part[0] * newer[..., None]
    return (summed, best, state[2] * older + part[2] * newer)


def cycle_pass(queries, keys, values, valid, move_queries, move_state):
    rows = queries.shape[0]
    state = (
        jnp.zeros((rows, HEADS, HD), jnp.float32),
        jnp.full((rows, HEADS), -jnp.inf, jnp.float32),
        jnp.zeros((rows, HEADS), jnp.float32),
    )

    def turn(step, carry):
        current, acc = carry
        acc = move_state(merge_state(acc, partial_scores(current, keys, values, valid)))
        return (move_queries(current), acc)

    current, state = lax.fori_loop(0, lax.axis_size("blk") - 1, turn, (queries, state))
    return move_state(merge_state(state, partial_scores(current, keys, values, valid)))


def session_attention(queries, keys, values, valid):
    rows = queries.shape[0]

    def ahead_queries(block):
        return passed_along(block, "blk", 1)

    def ahead_state(state):
        return passed_along(state, "blk", 1)

    state = cycle_pass(queries, keys, values, valid, ahead_queries, ahead_state)
    output = state[0] / state[2][..., None]
    return output.reshape(rows, HEADS * HD).astype(jnp.bfloat16)


def fetch_neighbours(cross, bank_kv, span_home, neighbours):
    spans = neighbours.shape[0]
    width = cross.shape[1]
    wanted = neighbours.reshape(-1)
    requests = wanted.shape[0]
    owners = lax.axis_size("bank")
    capacity = max(2, (requests + owners - 1) // owners)
    places = owners * capacity
    local_spans = bank_kv.shape[0]
    homes = jnp.take(span_home, wanted)
    owner = homes // local_spans
    local_slot = homes % local_spans
    hits = (owner[:, None] == jnp.arange(owners, dtype=jnp.int32)[None, :]).astype(jnp.int32)
    earlier = (jnp.arange(requests)[:, None] > jnp.arange(requests)[None, :]).astype(jnp.int32)
    rank = jnp.sum(jnp.dot(earlier, hits) * hits, axis=1)
    target = owner * capacity + rank
    placing = target[:, None] == jnp.arange(places, dtype=jnp.int32)[None, :]
    per_request = jnp.repeat(cross.reshape(spans, SPAN, width), NEIGH, axis=0)
    outgoing = jnp.einsum(
        "rs,rck->sck", placing.astype(jnp.bfloat16), per_request, preferred_element_type=jnp.float32
    ).astype(jnp.bfloat16)
    marks = jnp.sum(jnp.where(placing, local_slot[:, None], 0), axis=0).astype(jnp.bfloat16)
    outgoing = outgoing.reshape(owners, capacity, SPAN, width)
    marks = marks.reshape(owners, capacity)
    arrived, arrived_marks = (
        lax.all_to_all(outgoing, "bank", split_axis=0, concat_axis=0, tiled=True),
        lax.all_to_all(marks, "bank", split_axis=0, concat_axis=0, tiled=True),
    )
    flat_rows = arrived.reshape(owners * capacity * SPAN, width)
    row_marks = jnp.repeat(arrived_marks.reshape(-1).astype(jnp.int32), SPAN)
    bank_keys = bank_kv[:, :, :width].reshape(local_spans * NROW, width)
    bank_values = bank_kv[:, :, width:].reshape(local_spans * NROW, width)
    column_span = jnp.arange(local_spans * NROW, dtype=jnp.int32) // NROW
    valid = (row_marks[:, None] == column_span[None, :])[None]
    summed, top, total = partial_scores(flat_rows, bank_keys, bank_values, valid)
    normal = (summed / total[..., None]).astype(jnp.bfloat16).reshape(owners, capacity, SPAN, width)
    top = top.reshape(owners, capacity, SPAN, HEADS)
    total = total.reshape(owners, capacity, SPAN, HEADS)
    normal = lax.all_to_all(normal, "bank", split_axis=0, concat_axis=0, tiled=True)
    top, total = (
        lax.all_to_all(top, "bank", split_axis=0, concat_axis=0, tiled=True),
        lax.all_to_all(total, "bank", split_axis=0, concat_axis=0, tiled=True),
    )
    normal = jnp.take(normal.reshape(places, SPAN, width), target, axis=0)
    normal = normal.reshape(spans, NEIGH, SPAN, HEADS, HD).astype(jnp.float32)
    top = jnp.take(top.reshape(places, SPAN, HEADS), target, axis=0).reshape(
        spans, NEIGH, SPAN, HEADS
    )
    total = jnp.take(total.reshape(places, SPAN, HEADS), target, axis=0).reshape(
        spans, NEIGH, SPAN, HEADS
    )
    best = jnp.max(top, axis=1)
    weight = jnp.exp(top - best[:, None]) * total
    numer = jnp.sum(weight[..., None] * normal, axis=1)
    denom = jnp.sum(weight, axis=1)
    output = numer / denom[..., None]
    return output.reshape(spans * SPAN, width).astype(jnp.bfloat16)


HALF = HEADS // 2
HALF_WIDTH = HALF * HD


def put_logs(out_ref, logs):
    rows = logs.shape[0]
    lanes = pl.cdiv(rows, 128) * 128
    padded = jnp.concatenate((logs, jnp.zeros((lanes - rows, 128), jnp.float32)), axis=0)
    whole = jnp.transpose(padded)[:TAIL]
    first = whole.astype(jnp.bfloat16).astype(jnp.float32)
    rest = whole - first
    second = rest.astype(jnp.bfloat16).astype(jnp.float32)
    upper = lax.broadcasted_iota(jnp.int32, (TAIL, lanes), 0) < HALF
    out_ref[rows:, :lanes] = jnp.where(upper, first, rest - second).astype(jnp.bfloat16)
    out_ref[rows:, lanes : 2 * lanes] = second.astype(jnp.bfloat16)


def get_logs(part_ref):
    rows = part_ref.shape[0] - TAIL
    lanes = pl.cdiv(rows, 128) * 128
    first = part_ref[rows:, :lanes].astype(jnp.float32)
    second = part_ref[rows:, lanes : 2 * lanes].astype(jnp.float32)
    whole = (pltpu.roll(first, HALF, 0) + second) + first
    padded = jnp.concatenate((whole, jnp.zeros((128 - TAIL, lanes), jnp.float32)), axis=0)
    return jnp.transpose(padded)[:rows]


def head_columns(head):
    return slice(head * HD, (head + 1) * HD)


def attend(query_ref, key_ref, value_ref, filled_ref, half, out_ref):
    rows = out_ref.shape[0] - TAIL
    width = key_ref.shape[0]
    position = lax.broadcasted_iota(jnp.int32, (1, width), 1)
    hidden = jnp.where(position < filled_ref[0, 0], 0.0, FAR)
    lane = lax.broadcasted_iota(jnp.int32, (rows, 128), 1)
    tops = jnp.zeros((rows, 128), jnp.float32)
    totals = jnp.ones((rows, 128), jnp.float32)
    for place in range(HALF):
        columns = head_columns(half * HALF + place)
        if len(query_ref.shape) == 2:
            query = query_ref[:rows, columns]
        else:
            query = query_ref[half, :rows, head_columns(place)]
        scores = lax.dot_general(
            query,
            key_ref[:, columns],
            (((1,), (1,)), ((), ())),
            preferred_element_type=jnp.float32,
        )
        scores = scores * (HD ** (-0.5) * LOG2E) + hidden
        top = jnp.max(scores, axis=1, keepdims=True)
        expo = jnp.exp2(scores - top)
        total = jnp.sum(expo, axis=1, keepdims=True)
        summed = jnp.dot(
            expo.astype(jnp.bfloat16), value_ref[:, columns], preferred_element_type=jnp.float32
        )
        out_ref[:rows, head_columns(place)] = (summed * (1.0 / total)).astype(jnp.bfloat16)
        chosen = (lane == place) | (lane == place + HALF)
        tops = jnp.where(chosen, top, tops)
        totals = jnp.where(chosen, total, totals)
    put_logs(out_ref, tops + jnp.log(totals) * LOG2E)


def merge(refs, out_ref, columns, log_ref=None):
    rows = refs[0].shape[0] - TAIL
    logs = [get_logs(ref) for ref in refs]
    best = logs[0]
    for log in logs[1:]:
        best = jnp.maximum(best, log)
    factors = [jnp.exp2(log - best) for log in logs]
    total = sum(factors[1:], factors[0])
    if log_ref is not None:
        put_logs(log_ref, best + jnp.log(total) * LOG2E)
    inverse = 1.0 / total
    factors = [factor * inverse for factor in factors]
    for place in range(HALF):
        terms = [
            ref[:rows, head_columns(place)].astype(jnp.float32) * factor[:, place : place + 1]
            for ref, factor in zip(refs, factors)
        ]
        joined = sum(terms[1:], terms[0]).astype(jnp.bfloat16)
        out_ref[:rows, slice(columns + place * HD, columns + (place + 1) * HD)] = joined


def is_outer():
    place = lax.axis_index("blk")
    return (place == 0) | (place == lax.axis_size("blk") - 1)


def when_outer(body):
    pl.when(is_outer())(body)


def when_inner(body):
    pl.when(jnp.logical_not(is_outer()))(body)


def whole_kernel(filled_ref, query_ref, key_ref, value_ref, out_ref):
    for half in range(2):
        attend(query_ref, key_ref, value_ref, filled_ref, half, out_ref.at[half])


def outer_kernel(*refs):
    @when_outer
    def _():
        whole_kernel(*refs)


def far_kernel(filled_ref, query_ref, key_ref, value_ref, middle_ref, out_ref):
    @when_outer
    def _():
        whole_kernel(filled_ref, query_ref, key_ref, value_ref, out_ref)

    @when_inner
    def _():
        rows = middle_ref.shape[0]
        for half in range(2):
            out_ref[half, :rows] = middle_ref[:, half * HALF_WIDTH : (half + 1) * HALF_WIDTH]
            out_ref[half, rows:] = jnp.zeros((TAIL, HALF_WIDTH), jnp.bfloat16)


def inner_kernel(*refs):
    @when_inner
    def _():
        whole_kernel(*refs)


def meet_kernel(own_ref, other_ref, out_ref):
    @when_inner
    def _():
        for half in range(2):
            merge((own_ref.at[half], other_ref.at[half]), out_ref.at[half], 0, out_ref.at[half])


def join_kernel(own_ref, other_ref, out_ref):
    @when_outer
    def _():
        out_ref[...] = own_ref[...]

    @when_inner
    def _():
        for half in range(2):
            merge((own_ref.at[half], other_ref.at[half]), out_ref.at[half], 0, out_ref.at[half])


def closing_kernel(own_ref, side_ref, middle_ref, out_ref):
    @when_outer
    def _():
        for half in range(2):
            merge((own_ref.at[half], side_ref.at[half]), out_ref, half * HALF_WIDTH)

    @when_inner
    def _():
        for half in range(2):
            parts = (own_ref.at[half], side_ref.at[half], middle_ref.at[half])
            merge(parts, out_ref, half * HALF_WIDTH)


def spans_kernel(home_ref, wanted_ref, cross_ref, *refs):
    own_ref, core_ref, others_ref, core_others_ref, out_ref, bank_ref, arrivals = refs
    sources = [own_ref, core_ref]
    for place in range(3):
        sources += [others_ref.at[place], core_others_ref.at[place]]
    spans = wanted_ref.shape[1]
    held = bank_ref.shape[1]
    width = cross_ref.shape[1]
    copies = [
        pltpu.make_async_copy(source, bank_ref.at[place], arrivals.at[place])
        for place, source in enumerate(sources)
    ]
    for copy in copies:
        copy.start()
    for copy in copies:
        copy.wait()
    here = lax.axis_index("bank")
    row_head = lax.broadcasted_iota(jnp.int32, (HEADS * SPAN, width), 0) // SPAN
    column_head = lax.broadcasted_iota(jnp.int32, (HEADS * SPAN, width), 1) // HD
    mine = row_head == column_head

    def one_span(span, carry):
        start = pl.multiple_of(span * SPAN, SPAN)
        query = cross_ref[pl.ds(start, SPAN), :]
        spread = jnp.concatenate([query] * HEADS, axis=0)
        spread = jnp.where(mine, spread, jnp.zeros_like(spread))
        pairs = []
        for which in range(NEIGH):
            home = home_ref[wanted_ref[which, span]]
            owner = home // held
            pairs.append((owner ^ here, home - owner * held))
        keys = jnp.concatenate([bank_ref[place, slot, :, :width] for place, slot in pairs], axis=0)
        values = jnp.concatenate([bank_ref[place, slot, :, width:] for place, slot in pairs], axis=0)
        scores = lax.dot_general(
            spread, keys, (((1,), (1,)), ((), ())), preferred_element_type=jnp.float32
        ) * (HD ** (-0.5) * LOG2E)
        top = jnp.max(scores, axis=1, keepdims=True)
        expo = jnp.exp2(scores - top)
        total = jnp.sum(expo, axis=1, keepdims=True)
        weights = (expo * (1.0 / total)).astype(jnp.bfloat16)
        for head in range(HEADS):
            columns = head_columns(head)
            out_ref[pl.ds(start, SPAN), columns] = jnp.dot(
                weights[head * SPAN : (head + 1) * SPAN],
                values[:, columns],
                preferred_element_type=jnp.float32,
            ).astype(jnp.bfloat16)
        return carry

    lax.fori_loop(0, spans, one_span, 0, unroll=True)


SMALL = pl.BlockSpec(memory_space=pltpu.SMEM)
WHOLE = pl.BlockSpec(memory_space=pltpu.VMEM)
AWAY = pl.BlockSpec(memory_space=pl.ANY)


def on_core(kernel, shapes, in_specs, scratch=(), name=None):
    return pl.pallas_call(
        kernel,
        out_shape=shapes,
        in_specs=in_specs,
        out_specs=jax.tree.map(lambda _: WHOLE, shapes),
        scratch_shapes=scratch,
        cost_estimate=pl.CostEstimate(flops=1, transcendentals=0, bytes_accessed=1),
        compiler_params=pltpu.CompilerParams(vmem_limit_bytes=(10 if name == "spans" else 5) << 20),
        name=name,
    )


def after(block, *others):
    return lax.optimization_barrier((block, *others))[0]


def joint_pass(queries, keys, values, filled, cross, bank_kv, span_home, wanted):
    rows, width = queries.shape
    whole_part = jax.ShapeDtypeStruct((2, rows + TAIL, HALF_WIDTH), jnp.bfloat16)
    plain = jax.ShapeDtypeStruct((rows, width), jnp.bfloat16)

    def over_blk(block, *route):
        return lax.ppermute(block, "blk", route)

    def over_bank(block, distance):
        route = [(i, i ^ distance) for i in range(lax.axis_size("bank"))]
        return lax.ppermute(block, "bank", route)

    def attention(kernel, name, block):
        return on_core(kernel, whole_part, [SMALL] + [WHOLE] * 3, name=name)(filled, block, keys, values)

    swap_far = ((0, 3), (3, 0))
    swap_side = ((0, 1), (1, 0), (2, 3), (3, 2))
    swap_middle = ((1, 2), (2, 1))
    inward = ((0, 1), (3, 2))

    far = over_blk(queries, *swap_far)
    side = over_blk(queries, *swap_side)
    middle = over_blk(queries, *swap_middle)
    own = attention(whole_kernel, "own", queries)
    far_part = on_core(far_kernel, whole_part, [SMALL] + [WHOLE] * 4, name="far")(
        filled, after(far, own), keys, values, middle
    )
    crossed = over_blk(far_part, *swap_side)
    passed_in = over_blk(side, *swap_middle)
    bank_kv_late = after(bank_kv, far, own)
    bank_x = over_bank(bank_kv_late, 2)
    bank_y = over_bank(bank_kv_late, 4)
    bank_xy = over_bank(after(bank_kv_late, bank_x, bank_y), 6)
    side_part = attention(whole_kernel, "side", after(side, far_part, bank_x, bank_y))
    middle_part = attention(inner_kernel, "middle", after(middle, side_part))
    turned = attention(outer_kernel, "turned", after(crossed, passed_in, middle_part))
    from_outer = over_blk(turned, *inward)
    passed = attention(inner_kernel, "passed", after(passed_in, turned))
    met = on_core(meet_kernel, whole_part, [WHOLE] * 2, name="met")(passed, crossed)
    from_middle = over_blk(met, *swap_middle)
    join = on_core(join_kernel, whole_part, [WHOLE] * 2, name="join")
    to_middle = join(middle_part, from_outer)
    home_middle = over_blk(to_middle, *swap_middle)
    to_side = join(after(side_part, to_middle), from_middle)
    home_side = over_blk(to_side, *swap_side)
    core_c = over_bank(after(bank_kv, met), 1)
    others = after(jnp.stack((bank_x, bank_y, bank_xy)), to_side)
    core_others = over_bank(others, 1)

    retrieved = on_core(
        spans_kernel,
        plain,
        [SMALL, SMALL, WHOLE] + [AWAY] * 4,
        scratch=(pltpu.VMEM((8, *bank_kv.shape), bank_kv.dtype), pltpu.SemaphoreType.DMA((8,))),
        name="spans",
    )(span_home, wanted.T, after(cross, to_side), bank_kv, core_c, others, core_others)
    context = on_core(closing_kernel, plain, [WHOLE] * 3, name="closing")(
        after(own, retrieved), home_side, home_middle
    )
    return context, retrieved


def on_device(
    self_queries,
    cache_keys,
    cache_values,
    cache_lengths,
    cross_queries,
    bank_kv,
    span_home,
    neighbours,
):
    queries = self_queries[0]
    keys = cache_keys[0]
    values = cache_values[0]
    valid = (jnp.arange(keys.shape[0], dtype=jnp.int32) < cache_lengths[0, 0])[None, None, :]
    if lax.axis_size("blk") == 4 and lax.axis_size("bank") == 8:
        context, retrieved = joint_pass(
            queries, keys, values, cache_lengths, cross_queries[0], bank_kv, span_home, neighbours[0]
        )
        return (context[None], retrieved[None])
    context = session_attention(queries, keys, values, valid)
    retrieved = fetch_neighbours(cross_queries[0], bank_kv, span_home, neighbours[0])
    return (context[None], retrieved[None])


def solution(mesh):
    return jax.shard_map(
        on_device,
        mesh=mesh,
        in_specs=(
            P("bank", "blk", None),
            P("bank", "blk", None),
            P("bank", "blk", None),
            P("bank", "blk"),
            P("bank", "blk", None),
            P("bank", None, None),
            P(),
            P("bank", "blk", None),
        ),
        out_specs=(P("bank", "blk", None), P("bank", "blk", None)),
        check_vma=False,
    )
```

```python
import functools

import jax
import jax.numpy as jnp
from jax import lax
from jax.experimental import pallas as pl
from jax.experimental.pallas import tpu as pltpu
from jax.sharding import PartitionSpec as P

HEADS = 8
HD = 128
SPAN = 16
NROW = 64
NEIGH = 2
TAIL = 8
LOG2E = 1.4426950408889634
LN2 = 0.6931471805599453
FAR = -1e30


def passed_along(block, axis, distance):
    devices = range(lax.axis_size(axis))
    route = [((i - distance) % len(devices), i) for i in devices]
    return lax.ppermute(block, axis, route)


def partial_scores(queries, keys, values, valid):
    rows = queries.shape[0]
    width = keys.shape[0]
    query_heads = queries.reshape(rows, HEADS, HD)
    key_heads = keys.reshape(width, HEADS, HD)
    value_heads = values.reshape(width, HEADS, HD)
    scores = jnp.einsum(
        "rhd,chd->hrc", query_heads, key_heads, preferred_element_type=jnp.float32
    ) * HD ** (-0.5)
    scores = jnp.where(valid, scores, -jnp.inf)
    top = jnp.max(scores, axis=2)
    expo = jnp.exp(scores - top[:, :, None])
    total = jnp.sum(expo, axis=2)
    weights = expo.astype(jnp.bfloat16)
    summed = jnp.einsum("hrc,chd->rhd", weights, value_heads, preferred_element_type=jnp.float32)
    return (summed, top.T, total.T)


def merge_state(state, part):
    best = jnp.maximum(state[1], part[1])
    older = jnp.exp(state[1] - best)
    newer = jnp.exp(part[1] - best)
    summed = state[0] * older[..., None] + part[0] * newer[..., None]
    return (summed, best, state[2] * older + part[2] * newer)


def cycle_pass(queries, keys, values, valid, move_queries, move_state):
    rows = queries.shape[0]
    state = (
        jnp.zeros((rows, HEADS, HD), jnp.float32),
        jnp.full((rows, HEADS), -jnp.inf, jnp.float32),
        jnp.zeros((rows, HEADS), jnp.float32),
    )

    def turn(step, carry):
        current, acc = carry
        acc = move_state(merge_state(acc, partial_scores(current, keys, values, valid)))
        return (move_queries(current), acc)

    current, state = lax.fori_loop(0, lax.axis_size("blk") - 1, turn, (queries, state))
    return move_state(merge_state(state, partial_scores(current, keys, values, valid)))


def session_attention(queries, keys, values, valid):
    rows = queries.shape[0]

    def ahead_queries(block):
        return passed_along(block, "blk", 1)

    def ahead_state(state):
        return passed_along(state, "blk", 1)

    state = cycle_pass(queries, keys, values, valid, ahead_queries, ahead_state)
    output = state[0] / state[2][..., None]
    return output.reshape(rows, HEADS * HD).astype(jnp.bfloat16)


def fetch_neighbours(cross, bank_kv, span_home, neighbours):
    spans = neighbours.shape[0]
    width = cross.shape[1]
    wanted = neighbours.reshape(-1)
    requests = wanted.shape[0]
    owners = lax.axis_size("bank")
    capacity = max(2, (requests + owners - 1) // owners)
    places = owners * capacity
    local_spans = bank_kv.shape[0]
    homes = jnp.take(span_home, wanted)
    owner = homes // local_spans
    local_slot = homes % local_spans
    hits = (owner[:, None] == jnp.arange(owners, dtype=jnp.int32)[None, :]).astype(jnp.int32)
    earlier = (jnp.arange(requests)[:, None] > jnp.arange(requests)[None, :]).astype(jnp.int32)
    rank = jnp.sum(jnp.dot(earlier, hits) * hits, axis=1)
    target = owner * capacity + rank
    placing = target[:, None] == jnp.arange(places, dtype=jnp.int32)[None, :]
    per_request = jnp.repeat(cross.reshape(spans, SPAN, width), NEIGH, axis=0)
    outgoing = jnp.einsum(
        "rs,rck->sck", placing.astype(jnp.bfloat16), per_request, preferred_element_type=jnp.float32
    ).astype(jnp.bfloat16)
    marks = jnp.sum(jnp.where(placing, local_slot[:, None], 0), axis=0).astype(jnp.bfloat16)
    outgoing = outgoing.reshape(owners, capacity, SPAN, width)
    marks = marks.reshape(owners, capacity)
    arrived, arrived_marks = (
        lax.all_to_all(outgoing, "bank", split_axis=0, concat_axis=0, tiled=True),
        lax.all_to_all(marks, "bank", split_axis=0, concat_axis=0, tiled=True),
    )
    flat_rows = arrived.reshape(owners * capacity * SPAN, width)
    row_marks = jnp.repeat(arrived_marks.reshape(-1).astype(jnp.int32), SPAN)
    bank_keys = bank_kv[:, :, :width].reshape(local_spans * NROW, width)
    bank_values = bank_kv[:, :, width:].reshape(local_spans * NROW, width)
    column_span = jnp.arange(local_spans * NROW, dtype=jnp.int32) // NROW
    valid = (row_marks[:, None] == column_span[None, :])[None]
    summed, top, total = partial_scores(flat_rows, bank_keys, bank_values, valid)
    normal = (summed / total[..., None]).astype(jnp.bfloat16).reshape(owners, capacity, SPAN, width)
    top = top.reshape(owners, capacity, SPAN, HEADS)
    total = total.reshape(owners, capacity, SPAN, HEADS)
    normal = lax.all_to_all(normal, "bank", split_axis=0, concat_axis=0, tiled=True)
    top, total = (
        lax.all_to_all(top, "bank", split_axis=0, concat_axis=0, tiled=True),
        lax.all_to_all(total, "bank", split_axis=0, concat_axis=0, tiled=True),
    )
    normal = jnp.take(normal.reshape(places, SPAN, width), target, axis=0)
    normal = normal.reshape(spans, NEIGH, SPAN, HEADS, HD).astype(jnp.float32)
    top = jnp.take(top.reshape(places, SPAN, HEADS), target, axis=0).reshape(
        spans, NEIGH, SPAN, HEADS
    )
    total = jnp.take(total.reshape(places, SPAN, HEADS), target, axis=0).reshape(
        spans, NEIGH, SPAN, HEADS
    )
    best = jnp.max(top, axis=1)
    weight = jnp.exp(top - best[:, None]) * total
    numer = jnp.sum(weight[..., None] * normal, axis=1)
    denom = jnp.sum(weight, axis=1)
    output = numer / denom[..., None]
    return output.reshape(spans * SPAN, width).astype(jnp.bfloat16)


HALF = HEADS // 2
HALF_WIDTH = HALF * HD


def padded_lanes(rows):
    return pl.cdiv(rows, 128) * 128


def put_logs(out_ref, logs):
    rows = out_ref.shape[1] - TAIL
    lanes = logs.shape[1]
    first = logs.astype(jnp.bfloat16).astype(jnp.float32)
    rest = logs - first
    second = rest.astype(jnp.bfloat16).astype(jnp.float32)
    out_ref[0, rows:, :lanes] = first.astype(jnp.bfloat16)
    out_ref[0, rows:, lanes : 2 * lanes] = second.astype(jnp.bfloat16)
    out_ref[1, rows:, :lanes] = (rest - second).astype(jnp.bfloat16)
    out_ref[1, rows:, lanes : 2 * lanes] = jnp.zeros((TAIL, lanes), jnp.bfloat16)


def get_logs(part_ref):
    rows = part_ref.shape[1] - TAIL
    lanes = padded_lanes(rows)
    first = part_ref[0, rows:, :lanes].astype(jnp.float32)
    second = part_ref[0, rows:, lanes : 2 * lanes].astype(jnp.float32)
    third = part_ref[1, rows:, :lanes].astype(jnp.float32)
    return (third + second) + first


def head_columns(head):
    return slice(head * HD, (head + 1) * HD)


def head_place(head):
    return head // HALF, head_columns(head % HALF)


def attend(query_ref, key_ref, value_ref, filled_ref, out_ref):
    rows = out_ref.shape[1] - TAIL
    width = key_ref.shape[0]
    position = lax.broadcasted_iota(jnp.int32, (1, width), 1)
    hidden = jnp.where(position < filled_ref[0, 0], 0.0, FAR)
    lane = lax.broadcasted_iota(jnp.int32, (rows, 128), 1)

    def score(head):
        half, columns = head_place(head)
        if len(query_ref.shape) == 3:
            query = query_ref[half, :rows, columns]
        else:
            query = query_ref[:, head_columns(head)]
        return lax.dot_general(
            query,
            key_ref[:, head_columns(head)],
            (((1,), (1,)), ((), ())),
            preferred_element_type=jnp.float32,
        )

    def finish(head, weights, total):
        half, columns = head_place(head)
        summed = jnp.dot(weights, value_ref[:, head_columns(head)], preferred_element_type=jnp.float32)
        out_ref[half, :rows, columns] = (summed * (1.0 / total)).astype(jnp.bfloat16)

    ready = [score(0), score(1)]
    late = None
    tops = jnp.zeros((rows, 128), jnp.float32)
    totals = jnp.ones((rows, 128), jnp.float32)
    for head in range(HEADS):
        if head + 2 < HEADS:
            ready.append(score(head + 2))
        scores = ready.pop(0) * (HD ** (-0.5) * LOG2E) + hidden
        top = jnp.max(scores, axis=1, keepdims=True)
        expo = jnp.exp2(scores - top)
        total = jnp.sum(expo, axis=1, keepdims=True)
        if late is not None:
            finish(*late)
        late = (head, expo.astype(jnp.bfloat16), total)
        tops = jnp.where(lane == head, top, tops)
        totals = jnp.where(lane == head, total, totals)
    finish(*late)
    logs = tops + jnp.log(totals) * LOG2E
    lanes = padded_lanes(rows)
    if lanes > rows:
        logs = jnp.concatenate((logs, jnp.zeros((lanes - rows, 128), jnp.float32)), axis=0)
    put_logs(out_ref, jnp.transpose(logs)[:HEADS])


def merge(refs, put, log_ref=None):
    rows = refs[0].shape[1] - TAIL
    logs = [get_logs(ref) for ref in refs]
    best = logs[0]
    for log in logs[1:]:
        best = jnp.maximum(best, log)
    factors = [jnp.exp2(log - best) for log in logs]
    total = sum(factors[1:], factors[0])
    if log_ref is not None:
        put_logs(log_ref, best + jnp.log(total) * LOG2E)
    inverse = 1.0 / total
    factors = [factor * inverse for factor in factors]
    missing = 128 - HEADS * len(factors)
    factors.append(jnp.zeros((missing, factors[0].shape[1]), jnp.float32))
    columns = jnp.transpose(jnp.concatenate(factors, axis=0))[:rows]
    for head in range(HEADS):
        half, place = head_place(head)
        joined = None
        for which, ref in enumerate(refs):
            lane = which * HEADS + head
            term = ref[half, :rows, place].astype(jnp.float32) * columns[:, lane : lane + 1]
            joined = term if joined is None else joined + term
        put(head, joined.astype(jnp.bfloat16))


def merge_packed(refs, out_ref):
    rows = out_ref.shape[1] - TAIL

    def put(head, block):
        half, place = head_place(head)
        out_ref[half, :rows, place] = block

    merge(refs, put, out_ref)


def is_outer():
    place = lax.axis_index("blk")
    return (place == 0) | (place == lax.axis_size("blk") - 1)


def when_outer(body):
    pl.when(is_outer())(body)


def when_inner(body):
    pl.when(jnp.logical_not(is_outer()))(body)


def whole_kernel(filled_ref, query_ref, key_ref, value_ref, out_ref):
    attend(query_ref, key_ref, value_ref, filled_ref, out_ref)


def outer_kernel(*refs):
    @when_outer
    def _():
        whole_kernel(*refs)


def far_kernel(filled_ref, query_ref, key_ref, value_ref, middle_ref, out_ref):
    @when_outer
    def _():
        whole_kernel(filled_ref, query_ref, key_ref, value_ref, out_ref)

    @when_inner
    def _():
        rows = middle_ref.shape[0]
        for half in range(2):
            out_ref[half, :rows] = middle_ref[:, half * HALF_WIDTH : (half + 1) * HALF_WIDTH]
            out_ref[half, rows:] = jnp.zeros((TAIL, HALF_WIDTH), jnp.bfloat16)


def inner_kernel(*refs):
    @when_inner
    def _():
        whole_kernel(*refs)


def meet_kernel(own_ref, other_ref, out_ref):
    @when_inner
    def _():
        merge_packed((own_ref, other_ref), out_ref)


def join_kernel(own_ref, other_ref, out_ref):
    @when_outer
    def _():
        out_ref[...] = own_ref[...]

    @when_inner
    def _():
        merge_packed((own_ref, other_ref), out_ref)


def closing_kernel(own_ref, side_ref, middle_ref, out_ref):
    def put(head, block):
        out_ref[:, head_columns(head)] = block

    @when_outer
    def _():
        merge((own_ref, side_ref), put)

    @when_inner
    def _():
        merge((own_ref, side_ref, middle_ref), put)


def spans_kernel(home_ref, wanted_ref, cross_ref, *refs):
    own_ref, core_ref, others_ref, core_others_ref, out_ref, bank_ref, arrivals = refs
    sources = [own_ref, core_ref]
    for place in range(3):
        sources += [others_ref.at[place], core_others_ref.at[place]]
    spans = wanted_ref.shape[1]
    held = bank_ref.shape[1]
    width = cross_ref.shape[1]
    copies = [
        pltpu.make_async_copy(source, bank_ref.at[place], arrivals.at[place])
        for place, source in enumerate(sources)
    ]
    for copy in copies:
        copy.start()
    for copy in copies:
        copy.wait()
    here = lax.axis_index("bank")
    row_head = lax.broadcasted_iota(jnp.int32, (HEADS * SPAN, width), 0) // SPAN
    column_head = lax.broadcasted_iota(jnp.int32, (HEADS * SPAN, width), 1) // HD
    mine = row_head == column_head

    def one_span(span, carry):
        start = pl.multiple_of(span * SPAN, SPAN)
        query = cross_ref[pl.ds(start, SPAN), :]
        spread = jnp.concatenate([query] * HEADS, axis=0)
        spread = jnp.where(mine, spread, jnp.zeros_like(spread))
        pairs = []
        for which in range(NEIGH):
            home = home_ref[wanted_ref[which, span]]
            owner = home // held
            pairs.append((owner ^ here, home - owner * held))
        keys = jnp.concatenate([bank_ref[place, slot, :, :width] for place, slot in pairs], axis=0)
        values = jnp.concatenate([bank_ref[place, slot, :, width:] for place, slot in pairs], axis=0)
        scores = lax.dot_general(
            spread, keys, (((1,), (1,)), ((), ())), preferred_element_type=jnp.float32
        ) * (HD ** (-0.5) * LOG2E)
        top = jnp.max(scores, axis=1, keepdims=True)
        expo = jnp.exp2(scores - top)
        total = jnp.sum(expo, axis=1, keepdims=True)
        weights = (expo * (1.0 / total)).astype(jnp.bfloat16)
        for head in range(HEADS):
            columns = head_columns(head)
            out_ref[pl.ds(start, SPAN), columns] = jnp.dot(
                weights[head * SPAN : (head + 1) * SPAN],
                values[:, columns],
                preferred_element_type=jnp.float32,
            ).astype(jnp.bfloat16)
        return carry

    lax.fori_loop(0, spans, one_span, 0, unroll=True)


SMALL = pl.BlockSpec(memory_space=pltpu.SMEM)
WHOLE = pl.BlockSpec(memory_space=pltpu.VMEM)
AWAY = pl.BlockSpec(memory_space=pl.ANY)


def on_core(kernel, shapes, in_specs, scratch=(), name=None):
    return pl.pallas_call(
        kernel,
        out_shape=shapes,
        in_specs=in_specs,
        out_specs=jax.tree.map(lambda _: WHOLE, shapes),
        scratch_shapes=scratch,
        cost_estimate=pl.CostEstimate(flops=1, transcendentals=0, bytes_accessed=1),
        compiler_params=pltpu.CompilerParams(vmem_limit_bytes=(10 if name == "spans" else 5) << 20),
        name=name,
    )


def after(block, *others):
    return lax.optimization_barrier((block, *others))[0]


def joint_pass(queries, keys, values, filled, cross, bank_kv, span_home, wanted):
    rows, width = queries.shape
    whole_part = jax.ShapeDtypeStruct((2, rows + TAIL, HALF_WIDTH), jnp.bfloat16)
    plain = jax.ShapeDtypeStruct((rows, width), jnp.bfloat16)

    def over_blk(block, *route):
        return lax.ppermute(block, "blk", route)

    def over_bank(block, distance):
        route = [(i, i ^ distance) for i in range(lax.axis_size("bank"))]
        return lax.ppermute(block, "bank", route)

    def attention(kernel, name, block):
        return on_core(kernel, whole_part, [SMALL] + [WHOLE] * 3, name=name)(filled, block, keys, values)

    swap_far = ((0, 3), (3, 0))
    swap_side = ((0, 1), (1, 0), (2, 3), (3, 2))
    swap_middle = ((1, 2), (2, 1))
    inward = ((0, 1), (3, 2))

    far = over_blk(queries, *swap_far)
    side = over_blk(queries, *swap_side)
    middle = over_blk(queries, *swap_middle)
    own = attention(whole_kernel, "own", queries)
    far_part = on_core(far_kernel, whole_part, [SMALL] + [WHOLE] * 4, name="far")(
        filled, after(far, own), keys, values, middle
    )
    crossed = over_blk(far_part, *swap_side)
    passed_in = over_blk(side, *swap_middle)
    bank_kv_late = after(bank_kv, far, own)
    bank_x = over_bank(bank_kv_late, 2)
    bank_y = over_bank(bank_kv_late, 4)
    bank_xy = over_bank(after(bank_kv_late, bank_x, bank_y), 6)
    side_part = attention(whole_kernel, "side", after(side, far_part, bank_x, bank_y))
    middle_part = attention(inner_kernel, "middle", after(middle, side_part))
    turned = attention(outer_kernel, "turned", after(crossed, passed_in, middle_part))
    from_outer = over_blk(turned, *inward)
    passed = attention(inner_kernel, "passed", after(passed_in, turned))
    met = on_core(meet_kernel, whole_part, [WHOLE] * 2, name="met")(passed, crossed)
    from_middle = over_blk(met, *swap_middle)
    join = on_core(join_kernel, whole_part, [WHOLE] * 2, name="join")
    to_middle = join(middle_part, from_outer)
    home_middle = over_blk(to_middle, *swap_middle)
    to_side = join(after(side_part, to_middle), from_middle)
    home_side = over_blk(to_side, *swap_side)
    core_c = over_bank(after(bank_kv, met), 1)
    others = after(jnp.stack((bank_x, bank_y, bank_xy)), to_side)
    core_others = over_bank(others, 1)

    retrieved = on_core(
        spans_kernel,
        plain,
        [SMALL, SMALL, WHOLE] + [AWAY] * 4,
        scratch=(pltpu.VMEM((8, *bank_kv.shape), bank_kv.dtype), pltpu.SemaphoreType.DMA((8,))),
        name="spans",
    )(span_home, wanted.T, after(cross, to_side), bank_kv, core_c, others, core_others)
    context = on_core(closing_kernel, plain, [WHOLE] * 3, name="closing")(
        after(own, retrieved), home_side, home_middle
    )
    return context, retrieved


def on_device(
    self_queries,
    cache_keys,
    cache_values,
    cache_lengths,
    cross_queries,
    bank_kv,
    span_home,
    neighbours,
):
    queries = self_queries[0]
    keys = cache_keys[0]
    values = cache_values[0]
    valid = (jnp.arange(keys.shape[0], dtype=jnp.int32) < cache_lengths[0, 0])[None, None, :]
    if lax.axis_size("blk") == 4 and lax.axis_size("bank") == 8:
        context, retrieved = joint_pass(
            queries, keys, values, cache_lengths, cross_queries[0], bank_kv, span_home, neighbours[0]
        )
        return (context[None], retrieved[None])
    context = session_attention(queries, keys, values, valid)
    retrieved = fetch_neighbours(cross_queries[0], bank_kv, span_home, neighbours[0])
    return (context[None], retrieved[None])


def solution(mesh):
    return jax.shard_map(
        on_device,
        mesh=mesh,
        in_specs=(
            P("bank", "blk", None),
            P("bank", "blk", None),
            P("bank", "blk", None),
            P("bank", "blk"),
            P("bank", "blk", None),
            P("bank", None, None),
            P(),
            P("bank", "blk", None),
        ),
        out_specs=(P("bank", "blk", None), P("bank", "blk", None)),
        check_vma=False,
    )
```

```python
import functools

import jax
import jax.numpy as jnp
from jax import lax
from jax.experimental import pallas as pl
from jax.experimental.pallas import tpu as pltpu
from jax.sharding import PartitionSpec as P

HEADS = 8
HD = 128
SPAN = 16
NROW = 64
NEIGH = 2
TAIL = 8
LOG2E = 1.4426950408889634
LN2 = 0.6931471805599453
FAR = -1e30


def passed_along(block, axis, distance):
    devices = range(lax.axis_size(axis))
    route = [((i - distance) % len(devices), i) for i in devices]
    return lax.ppermute(block, axis, route)


def partial_scores(queries, keys, values, valid):
    rows = queries.shape[0]
    width = keys.shape[0]
    query_heads = queries.reshape(rows, HEADS, HD)
    key_heads = keys.reshape(width, HEADS, HD)
    value_heads = values.reshape(width, HEADS, HD)
    scores = jnp.einsum(
        "rhd,chd->hrc", query_heads, key_heads, preferred_element_type=jnp.float32
    ) * HD ** (-0.5)
    scores = jnp.where(valid, scores, -jnp.inf)
    top = jnp.max(scores, axis=2)
    expo = jnp.exp(scores - top[:, :, None])
    total = jnp.sum(expo, axis=2)
    weights = expo.astype(jnp.bfloat16)
    summed = jnp.einsum("hrc,chd->rhd", weights, value_heads, preferred_element_type=jnp.float32)
    return (summed, top.T, total.T)


def merge_state(state, part):
    best = jnp.maximum(state[1], part[1])
    older = jnp.exp(state[1] - best)
    newer = jnp.exp(part[1] - best)
    summed = state[0] * older[..., None] + part[0] * newer[..., None]
    return (summed, best, state[2] * older + part[2] * newer)


def cycle_pass(queries, keys, values, valid, move_queries, move_state):
    rows = queries.shape[0]
    state = (
        jnp.zeros((rows, HEADS, HD), jnp.float32),
        jnp.full((rows, HEADS), -jnp.inf, jnp.float32),
        jnp.zeros((rows, HEADS), jnp.float32),
    )

    def turn(step, carry):
        current, acc = carry
        acc = move_state(merge_state(acc, partial_scores(current, keys, values, valid)))
        return (move_queries(current), acc)

    current, state = lax.fori_loop(0, lax.axis_size("blk") - 1, turn, (queries, state))
    return move_state(merge_state(state, partial_scores(current, keys, values, valid)))


def session_attention(queries, keys, values, valid):
    rows = queries.shape[0]

    def ahead_queries(block):
        return passed_along(block, "blk", 1)

    def ahead_state(state):
        return passed_along(state, "blk", 1)

    state = cycle_pass(queries, keys, values, valid, ahead_queries, ahead_state)
    output = state[0] / state[2][..., None]
    return output.reshape(rows, HEADS * HD).astype(jnp.bfloat16)


def fetch_neighbours(cross, bank_kv, span_home, neighbours):
    spans = neighbours.shape[0]
    width = cross.shape[1]
    wanted = neighbours.reshape(-1)
    requests = wanted.shape[0]
    owners = lax.axis_size("bank")
    capacity = max(2, (requests + owners - 1) // owners)
    places = owners * capacity
    local_spans = bank_kv.shape[0]
    homes = jnp.take(span_home, wanted)
    owner = homes // local_spans
    local_slot = homes % local_spans
    hits = (owner[:, None] == jnp.arange(owners, dtype=jnp.int32)[None, :]).astype(jnp.int32)
    earlier = (jnp.arange(requests)[:, None] > jnp.arange(requests)[None, :]).astype(jnp.int32)
    rank = jnp.sum(jnp.dot(earlier, hits) * hits, axis=1)
    target = owner * capacity + rank
    placing = target[:, None] == jnp.arange(places, dtype=jnp.int32)[None, :]
    per_request = jnp.repeat(cross.reshape(spans, SPAN, width), NEIGH, axis=0)
    outgoing = jnp.einsum(
        "rs,rck->sck", placing.astype(jnp.bfloat16), per_request, preferred_element_type=jnp.float32
    ).astype(jnp.bfloat16)
    marks = jnp.sum(jnp.where(placing, local_slot[:, None], 0), axis=0).astype(jnp.bfloat16)
    outgoing = outgoing.reshape(owners, capacity, SPAN, width)
    marks = marks.reshape(owners, capacity)
    arrived, arrived_marks = (
        lax.all_to_all(outgoing, "bank", split_axis=0, concat_axis=0, tiled=True),
        lax.all_to_all(marks, "bank", split_axis=0, concat_axis=0, tiled=True),
    )
    flat_rows = arrived.reshape(owners * capacity * SPAN, width)
    row_marks = jnp.repeat(arrived_marks.reshape(-1).astype(jnp.int32), SPAN)
    bank_keys = bank_kv[:, :, :width].reshape(local_spans * NROW, width)
    bank_values = bank_kv[:, :, width:].reshape(local_spans * NROW, width)
    column_span = jnp.arange(local_spans * NROW, dtype=jnp.int32) // NROW
    valid = (row_marks[:, None] == column_span[None, :])[None]
    summed, top, total = partial_scores(flat_rows, bank_keys, bank_values, valid)
    normal = (summed / total[..., None]).astype(jnp.bfloat16).reshape(owners, capacity, SPAN, width)
    top = top.reshape(owners, capacity, SPAN, HEADS)
    total = total.reshape(owners, capacity, SPAN, HEADS)
    normal = lax.all_to_all(normal, "bank", split_axis=0, concat_axis=0, tiled=True)
    top, total = (
        lax.all_to_all(top, "bank", split_axis=0, concat_axis=0, tiled=True),
        lax.all_to_all(total, "bank", split_axis=0, concat_axis=0, tiled=True),
    )
    normal = jnp.take(normal.reshape(places, SPAN, width), target, axis=0)
    normal = normal.reshape(spans, NEIGH, SPAN, HEADS, HD).astype(jnp.float32)
    top = jnp.take(top.reshape(places, SPAN, HEADS), target, axis=0).reshape(
        spans, NEIGH, SPAN, HEADS
    )
    total = jnp.take(total.reshape(places, SPAN, HEADS), target, axis=0).reshape(
        spans, NEIGH, SPAN, HEADS
    )
    best = jnp.max(top, axis=1)
    weight = jnp.exp(top - best[:, None]) * total
    numer = jnp.sum(weight[..., None] * normal, axis=1)
    denom = jnp.sum(weight, axis=1)
    output = numer / denom[..., None]
    return output.reshape(spans * SPAN, width).astype(jnp.bfloat16)


HALF = HEADS // 2
HALF_WIDTH = HALF * HD


def padded_lanes(rows):
    return pl.cdiv(rows, 128) * 128


def put_logs(out_ref, logs):
    rows = out_ref.shape[1] - TAIL
    lanes = logs.shape[1]
    first = logs.astype(jnp.bfloat16).astype(jnp.float32)
    rest = logs - first
    second = rest.astype(jnp.bfloat16).astype(jnp.float32)
    out_ref[0, rows:, :lanes] = first.astype(jnp.bfloat16)
    out_ref[0, rows:, lanes : 2 * lanes] = second.astype(jnp.bfloat16)
    out_ref[1, rows:, :lanes] = (rest - second).astype(jnp.bfloat16)
    out_ref[1, rows:, lanes : 2 * lanes] = jnp.zeros((TAIL, lanes), jnp.bfloat16)


def get_logs(part_ref):
    rows = part_ref.shape[1] - TAIL
    lanes = padded_lanes(rows)
    first = part_ref[0, rows:, :lanes].astype(jnp.float32)
    second = part_ref[0, rows:, lanes : 2 * lanes].astype(jnp.float32)
    third = part_ref[1, rows:, :lanes].astype(jnp.float32)
    return (third + second) + first


def head_columns(head):
    return slice(head * HD, (head + 1) * HD)


def head_place(head):
    return head // HALF, head_columns(head % HALF)


def attend(query_ref, key_ref, value_ref, filled_ref, out_ref):
    rows = out_ref.shape[1] - TAIL
    width = key_ref.shape[0]
    position = lax.broadcasted_iota(jnp.int32, (1, width), 1)
    hidden = jnp.where(position < filled_ref[0, 0], 0.0, FAR)
    lane = lax.broadcasted_iota(jnp.int32, (rows, 128), 1)

    def score(head):
        half, columns = head_place(head)
        if len(query_ref.shape) == 3:
            query = query_ref[half, :rows, columns]
        else:
            query = query_ref[:, head_columns(head)]
        return lax.dot_general(
            query,
            key_ref[:, head_columns(head)],
            (((1,), (1,)), ((), ())),
            preferred_element_type=jnp.float32,
        )

    def finish(head, weights, total):
        half, columns = head_place(head)
        summed = jnp.dot(weights, value_ref[:, head_columns(head)], preferred_element_type=jnp.float32)
        out_ref[half, :rows, columns] = (summed * (1.0 / total)).astype(jnp.bfloat16)

    ready = [score(0), score(1)]
    late = None
    tops = jnp.zeros((rows, 128), jnp.float32)
    totals = jnp.ones((rows, 128), jnp.float32)
    for head in range(HEADS):
        if head + 2 < HEADS:
            ready.append(score(head + 2))
        scores = ready.pop(0) * (HD ** (-0.5) * LOG2E) + hidden
        top = jnp.max(scores, axis=1, keepdims=True)
        expo = jnp.exp2(scores - top)
        total = jnp.sum(expo, axis=1, keepdims=True)
        if late is not None:
            finish(*late)
        late = (head, expo.astype(jnp.bfloat16), total)
        tops = jnp.where(lane == head, top, tops)
        totals = jnp.where(lane == head, total, totals)
    finish(*late)
    logs = tops + jnp.log(totals) * LOG2E
    lanes = padded_lanes(rows)
    if lanes > rows:
        logs = jnp.concatenate((logs, jnp.zeros((lanes - rows, 128), jnp.float32)), axis=0)
    put_logs(out_ref, jnp.transpose(logs)[:HEADS])


def merge(refs, put, log_ref=None):
    rows = refs[0].shape[1] - TAIL
    logs = [get_logs(ref) for ref in refs]
    best = logs[0]
    for log in logs[1:]:
        best = jnp.maximum(best, log)
    factors = [jnp.exp2(log - best) for log in logs]
    total = sum(factors[1:], factors[0])
    if log_ref is not None:
        put_logs(log_ref, best + jnp.log(total) * LOG2E)
    inverse = 1.0 / total
    factors = [factor * inverse for factor in factors]
    missing = 128 - HEADS * len(factors)
    factors.append(jnp.zeros((missing, factors[0].shape[1]), jnp.float32))
    columns = jnp.transpose(jnp.concatenate(factors, axis=0))[:rows]
    for head in range(HEADS):
        half, place = head_place(head)
        joined = None
        for which, ref in enumerate(refs):
            lane = which * HEADS + head
            term = ref[half, :rows, place].astype(jnp.float32) * columns[:, lane : lane + 1]
            joined = term if joined is None else joined + term
        put(head, joined.astype(jnp.bfloat16))


def merge_packed(refs, out_ref):
    rows = out_ref.shape[1] - TAIL

    def put(head, block):
        half, place = head_place(head)
        out_ref[half, :rows, place] = block

    merge(refs, put, out_ref)


def is_outer():
    place = lax.axis_index("blk")
    return (place == 0) | (place == lax.axis_size("blk") - 1)


def when_outer(body):
    pl.when(is_outer())(body)


def when_inner(body):
    pl.when(jnp.logical_not(is_outer()))(body)


def whole_kernel(filled_ref, query_ref, key_ref, value_ref, out_ref):
    attend(query_ref, key_ref, value_ref, filled_ref, out_ref)


def outer_kernel(*refs):
    @when_outer
    def _():
        whole_kernel(*refs)


def far_kernel(filled_ref, query_ref, key_ref, value_ref, middle_ref, out_ref):
    @when_outer
    def _():
        whole_kernel(filled_ref, query_ref, key_ref, value_ref, out_ref)

    @when_inner
    def _():
        rows = middle_ref.shape[0]
        for half in range(2):
            out_ref[half, :rows] = middle_ref[:, half * HALF_WIDTH : (half + 1) * HALF_WIDTH]
            out_ref[half, rows:] = jnp.zeros((TAIL, HALF_WIDTH), jnp.bfloat16)


def inner_kernel(*refs):
    @when_inner
    def _():
        whole_kernel(*refs)


def meet_kernel(own_ref, other_ref, out_ref):
    @when_inner
    def _():
        merge_packed((own_ref, other_ref), out_ref)


def join_kernel(own_ref, other_ref, out_ref):
    @when_outer
    def _():
        out_ref[...] = own_ref[...]

    @when_inner
    def _():
        merge_packed((own_ref, other_ref), out_ref)


def near_kernel(own_ref, side_ref, out_ref):
    merge_packed((own_ref, side_ref), out_ref)


def closing_kernel(near_ref, middle_ref, out_ref):
    def put(head, block):
        out_ref[:, head_columns(head)] = block

    @when_outer
    def _():
        for head in range(HEADS):
            half, place = head_place(head)
            put(head, near_ref[half, : out_ref.shape[0], place])

    @when_inner
    def _():
        merge((near_ref, middle_ref), put)


def spans_kernel(home_ref, wanted_ref, cross_ref, *refs):
    same_ref, other_ref, out_ref, bank_ref, arrivals = refs
    sources = []
    for place in range(4):
        sources += [same_ref.at[place], other_ref.at[place]]
    spans = wanted_ref.shape[1]
    held = bank_ref.shape[1]
    width = cross_ref.shape[1]
    copies = [
        pltpu.make_async_copy(source, bank_ref.at[place], arrivals.at[place])
        for place, source in enumerate(sources)
    ]
    for copy in copies:
        copy.start()
    for copy in copies:
        copy.wait()
    here = lax.axis_index("bank")
    row_head = lax.broadcasted_iota(jnp.int32, (HEADS * SPAN, width), 0) // SPAN
    column_head = lax.broadcasted_iota(jnp.int32, (HEADS * SPAN, width), 1) // HD
    mine = row_head == column_head

    def one_span(span, carry):
        start = pl.multiple_of(span * SPAN, SPAN)
        query = cross_ref[pl.ds(start, SPAN), :]
        spread = jnp.concatenate([query] * HEADS, axis=0)
        spread = jnp.where(mine, spread, jnp.zeros_like(spread))
        pairs = []
        for which in range(NEIGH):
            home = home_ref[wanted_ref[which, span]]
            owner = home // held
            pairs.append((owner ^ here, home - owner * held))
        keys = jnp.concatenate([bank_ref[place, slot, :, :width] for place, slot in pairs], axis=0)
        values = jnp.concatenate([bank_ref[place, slot, :, width:] for place, slot in pairs], axis=0)
        scores = lax.dot_general(
            spread, keys, (((1,), (1,)), ((), ())), preferred_element_type=jnp.float32
        ) * (HD ** (-0.5) * LOG2E)
        top = jnp.max(scores, axis=1, keepdims=True)
        expo = jnp.exp2(scores - top)
        total = jnp.sum(expo, axis=1, keepdims=True)
        weights = (expo * (1.0 / total)).astype(jnp.bfloat16)
        for head in range(HEADS):
            columns = head_columns(head)
            out_ref[pl.ds(start, SPAN), columns] = jnp.dot(
                weights[head * SPAN : (head + 1) * SPAN],
                values[:, columns],
                preferred_element_type=jnp.float32,
            ).astype(jnp.bfloat16)
        return carry

    lax.fori_loop(0, spans, one_span, 0, unroll=True)


SMALL = pl.BlockSpec(memory_space=pltpu.SMEM)
WHOLE = pl.BlockSpec(memory_space=pltpu.VMEM)
AWAY = pl.BlockSpec(memory_space=pl.ANY)


def on_core(kernel, shapes, in_specs, scratch=(), name=None):
    return pl.pallas_call(
        kernel,
        out_shape=shapes,
        in_specs=in_specs,
        out_specs=jax.tree.map(lambda _: WHOLE, shapes),
        scratch_shapes=scratch,
        cost_estimate=pl.CostEstimate(flops=1, transcendentals=0, bytes_accessed=1),
        compiler_params=pltpu.CompilerParams(vmem_limit_bytes=(10 if name == "spans" else 5) << 20),
        name=name,
    )


def after(block, *others):
    return lax.optimization_barrier((block, *others))[0]


def joint_pass(queries, keys, values, filled, cross, bank_kv, span_home, wanted):
    rows, width = queries.shape
    whole_part = jax.ShapeDtypeStruct((2, rows + TAIL, HALF_WIDTH), jnp.bfloat16)
    plain = jax.ShapeDtypeStruct((rows, width), jnp.bfloat16)

    def over_blk(block, *route):
        return lax.ppermute(block, "blk", route)

    def over_bank(block, distance):
        route = [(i, i ^ distance) for i in range(lax.axis_size("bank"))]
        return lax.ppermute(block, "bank", route)

    def attention(kernel, name, block):
        return on_core(kernel, whole_part, [SMALL] + [WHOLE] * 3, name=name)(filled, block, keys, values)

    swap_far = ((0, 3), (3, 0))
    swap_side = ((0, 1), (1, 0), (2, 3), (3, 2))
    swap_middle = ((1, 2), (2, 1))
    inward = ((0, 1), (3, 2))

    far = over_blk(queries, *swap_far)
    side = over_blk(queries, *swap_side)
    middle = over_blk(queries, *swap_middle)
    own = attention(whole_kernel, "own", queries)
    far_part = on_core(far_kernel, whole_part, [SMALL] + [WHOLE] * 4, name="far")(
        filled, after(far, own), keys, values, middle
    )
    crossed = over_blk(far_part, *swap_side)
    passed_in = over_blk(side, *swap_middle)
    bank_kv_late = after(bank_kv, far, own)
    bank_x = over_bank(bank_kv_late, 2)
    bank_y = over_bank(bank_kv_late, 4)
    bank_xy = over_bank(after(bank_kv_late, bank_x, bank_y), 6)
    side_part = attention(whole_kernel, "side", after(side, far_part, bank_x, bank_y))
    middle_part = attention(inner_kernel, "middle", after(middle, side_part))
    turned = attention(outer_kernel, "turned", after(crossed, passed_in, middle_part))
    from_outer = over_blk(turned, *inward)
    passed = attention(inner_kernel, "passed", after(passed_in, turned))
    met = on_core(meet_kernel, whole_part, [WHOLE] * 2, name="met")(passed, crossed)
    from_middle = over_blk(met, *swap_middle)
    join = on_core(join_kernel, whole_part, [WHOLE] * 2, name="join")
    to_middle = join(middle_part, from_outer)
    home_middle = over_blk(to_middle, *swap_middle)
    stacked = jnp.stack((bank_kv, bank_x, bank_y, bank_xy))
    to_side = join(after(side_part, to_middle, stacked), from_middle)
    home_side = over_blk(to_side, *swap_side)
    others = after(stacked, to_side)
    core_others = over_bank(others, 1)

    retrieved = on_core(
        spans_kernel,
        plain,
        [SMALL, SMALL, WHOLE] + [AWAY] * 2,
        scratch=(pltpu.VMEM((8, *bank_kv.shape), bank_kv.dtype), pltpu.SemaphoreType.DMA((8,))),
        name="spans",
    )(span_home, wanted.T, after(cross, to_side), stacked, core_others)
    partly = on_core(near_kernel, whole_part, [WHOLE] * 2, name="near")(after(own, retrieved), home_side)
    context = on_core(closing_kernel, plain, [WHOLE] * 2, name="closing")(partly, home_middle)
    return context, retrieved


def on_device(
    self_queries,
    cache_keys,
    cache_values,
    cache_lengths,
    cross_queries,
    bank_kv,
    span_home,
    neighbours,
):
    queries = self_queries[0]
    keys = cache_keys[0]
    values = cache_values[0]
    valid = (jnp.arange(keys.shape[0], dtype=jnp.int32) < cache_lengths[0, 0])[None, None, :]
    if lax.axis_size("blk") == 4 and lax.axis_size("bank") == 8:
        context, retrieved = joint_pass(
            queries, keys, values, cache_lengths, cross_queries[0], bank_kv, span_home, neighbours[0]
        )
        return (context[None], retrieved[None])
    context = session_attention(queries, keys, values, valid)
    retrieved = fetch_neighbours(cross_queries[0], bank_kv, span_home, neighbours[0])
    return (context[None], retrieved[None])


def solution(mesh):
    return jax.shard_map(
        on_device,
        mesh=mesh,
        in_specs=(
            P("bank", "blk", None),
            P("bank", "blk", None),
            P("bank", "blk", None),
            P("bank", "blk"),
            P("bank", "blk", None),
            P("bank", None, None),
            P(),
            P("bank", "blk", None),
        ),
        out_specs=(P("bank", "blk", None), P("bank", "blk", None)),
        check_vma=False,
    )
```
